32 devices in a mesh: parts: 2 (over y), ep: 16 (over z, x, core).
Axes of the slice: x: 2, y: 2, z: 4, core: 2. Of those that a mesh axis runs over, the one named last changes fastest.
Arguments:
- tokens: bfloat16 [512, 2048], P(('parts', 'ep')), parts along dimension 0, may hold values from -6 to 6
- gate_up: bfloat16 [4096, 16, 1536], P(('parts', 'ep')), parts along dimension 0, may hold values from -0.125 to 0.125
- down_proj: bfloat16 [1536, 16, 2048], P(('parts', 'ep')), parts along dimension 0, may hold values from -0.21875 to 0.21875
- expert_ids: int32 [512, 8], P(('parts', 'ep')), parts along dimension 0, may hold values from 0 to 15, all different within a row; in each aligned block of 16 rows (0 to 15, 16 to 31, ...) at most 16 rows name the same one
- gate_weights: float32 [512, 8], P(('parts', 'ep')), parts along dimension 0, may hold values from 0.03 to 0.6
- owner_slot: int32 [32], P('parts'), parts along dimension 0, may hold values from 0 to 15, each once
Outputs:
- moe_out: bfloat16 [512, 2048], P(('parts', 'ep')), parts along dimension 0
- channel_scale: float32 [32, 3584], P(('parts', 'ep')), parts along dimension 0
The draws below stay inside these ranges and needn't reach their ends.
There are 2 independent parts, one for each index of `parts`. The reference program is written for one: setup_inputs(seed, part) draws one part's arguments, and reference() takes and returns one part's arrays. A program takes and returns all parts, laid end to end along the dimension named above; each array names one. Nothing has to cross between parts.
Inputs may be any that keep to these rules, and one draw needn't show every extreme that they name: `expert_ids`: each row names 8 different experts; among the rows of one device no expert is named more than 16 times, a bound that some block reaches. `owner_slot`: A permutation: each slot holds exactly one expert.
All inputs are finite; a program needn't handle non-finite values.
Results may differ from the reference program's by a relative error of at most 0.0058.
Values may be sent and summed in bfloat16 or wider, within the bound.
No kernel may reach another device: no remote copies, remote signals or barrier semaphores. Data moves between devices by JAX's collectives and lax.ppermute only.
A program may use at most 128 MiB of HBM per device.

```python
import math
import jax
import jax.numpy as jnp
import numpy as np
from jax import lax

D = 2048
F = 768
TOPK = 8
TOK_DEV = 16
EXPERTS = 16
TOKENS = 256
CAP = 16
N_EP = 16


def levels(key, dims, cuts, low, largest):
    level, own = 1.0, jax.random.fold_in(key, 6)
    for position, shards_of in cuts:
        draws = jnp.exp(jax.random.uniform(jax.random.fold_in(own, position), (shards_of,), jnp.float32, low / len(cuts), largest / len(cuts)))
        level = level * jnp.repeat(draws, dims[position] // shards_of).reshape([-1 if axis == position else 1 for axis in range(len(dims))])
    return level


def deal_out(rng, own, number, rows, number_of, top, most, slope):
    order = jax.random.permutation(rng, number_of)
    packed, common = portions_of(number_of, rows * top, most, slope, True), portions_of(number_of, rows * top, most, slope, False)
    places = jnp.arange(number_of)

    def named(sizes, offset_by):
        used = int((sizes > 0).sum())
        fixed = max(1, used // 4)
        shifted = fixed + (places - fixed + offset_by * (used - fixed)) % max(1, number_of - fixed)
        return jnp.zeros((number_of,), jnp.int32).at[order[jnp.where(places < fixed, places, shifted)]].set(jnp.asarray(sizes, jnp.int32))

    sizes = jnp.where(number % 4 == 0, named(packed, number // 4), named(common, number - number // 4 - 1))
    mixed = jax.random.permutation(jax.random.fold_in(own, 3), number_of)
    source_of, sink = mixed[0:number_of // 2 * 2:2], mixed[1:number_of // 2 * 2:2]
    slack = jnp.minimum(sizes[source_of] - 1, most - sizes[sink]) // 2
    slack = jnp.where((source_of == order[0]) | (sink == order[0]) | (sizes[sink] == 0), 0, jnp.maximum(slack, 0))
    shifted = jax.random.randint(jax.random.fold_in(own, 4), (number_of // 2,), 0, 1 << 20) % (slack + 1)
    sizes = sizes.at[source_of].add(-shifted).at[sink].add(shifted)
    members = jnp.searchsorted(jnp.cumsum(sizes), jnp.arange(rows * top), side="right").astype(jnp.int32)
    listing = members.reshape(top, rows).T
    listing = listing[jax.random.permutation(jax.random.fold_in(own, 1), rows)]
    offset_by = jax.random.randint(jax.random.fold_in(own, 2), (rows, 1), 0, top)
    return jnp.take_along_axis(listing, (jnp.arange(top)[None, :] + offset_by) % top, axis=1)


def portions_of(amount, total, limit, lean, full):
    loads = [(1 << 20) // math.isqrt(grade ** lean) + 1 for grade in range(1, amount + 1)]
    largest = limit if full else min(limit, max(-(-total // amount), total * loads[0] // sum(loads)))
    least = 1 if total - largest >= amount - 1 else 0
    given, spare = [largest] + [least] * (amount - 1), total - largest - least * (amount - 1)
    while spare > 0:
        movable = [i for i in range(1, amount) if given[i] < largest] or [i for i in range(1, amount) if given[i] < limit]
        whole, budget = sum([loads[i] for i in movable]), spare
        for i in movable:
            more = min(limit - given[i], max(1, budget * loads[i] // whole), spare)
            given[i] = given[i] + more
            spare = spare - more
    return np.array(given)


def normal_values(key, shape, scale, most, cuts=(), held_as=jnp.bfloat16):
    factor_of = levels(key, shape, cuts, -0.22, 0.18) if cuts else 1.0
    values = jax.random.normal(key, shape, jnp.float32) * scale * factor_of
    return jnp.minimum(jnp.maximum(values, -most), most).astype(held_as)


def setup_inputs(seed: int = 0, part: int = 0) -> dict:
    key_list = jax.random.split(jax.random.key(seed), 7)
    part_splits = jax.random.split(jax.random.fold_in(key_list[6], part), 7)
    tokens = normal_values(part_splits[0], (TOKENS, D), 1.0, 6.0, ((0, 16),))
    gate_up = normal_values(part_splits[1], (D, EXPERTS, 2 * F), D ** -0.5, 0.125, ((0, 16),))
    down_proj = normal_values(part_splits[2], (F, EXPERTS, D), F ** -0.5, 0.21875, ((0, 16),))
    expert_ids_keys = jax.random.split(jax.random.fold_in(part_splits[3], 1), TOKENS // TOK_DEV)
    expert_ids_turns = jax.random.permutation(jax.random.fold_in(part_splits[3], 3), TOKENS // TOK_DEV)
    expert_ids = jax.vmap(lambda own, number: deal_out(jax.random.fold_in(part_splits[3], 2), own, number, TOK_DEV, EXPERTS, TOPK, CAP, 1))(expert_ids_keys, expert_ids_turns).reshape((TOKENS, TOPK))
    gate_weights = jnp.clip(jnp.exp(math.log(0.6) - 2.9957323 * jax.random.uniform(part_splits[4], (TOKENS, TOPK), jnp.float32) ** levels(part_splits[4], (TOKENS, TOPK), ((0, 16),), -0.2, 0.2)), 0.03, 0.6)
    owner_slot = jax.random.permutation(part_splits[5], EXPERTS).astype(jnp.int32)
    return dict(tokens=tokens, gate_up=gate_up, down_proj=down_proj, expert_ids=expert_ids, gate_weights=gate_weights, owner_slot=owner_slot)


def expert_ffn(rows, w_up, w_down):
    hidden = jnp.dot(rows, w_up, preferred_element_type=jnp.float32)
    ffn_width = w_up.shape[1] // 2
    activated = (jax.nn.silu(hidden[:, :ffn_width]) * hidden[:, ffn_width:]).astype(jnp.bfloat16)
    return jnp.dot(activated, w_down, preferred_element_type=jnp.float32).astype(jnp.bfloat16)

def column_scales(gate_up, down_proj):
    gate_scale = lax.optimization_barrier(jnp.max(jnp.abs(gate_up), axis=0)).astype(jnp.float32) * math.sqrt(gate_up.shape[0])
    down_scale = lax.optimization_barrier(jnp.max(jnp.abs(down_proj), axis=0)).astype(jnp.float32) * math.sqrt(down_proj.shape[0])
    return jnp.concatenate([gate_scale, down_scale], axis=1)

def reference(tokens, gate_up, down_proj, expert_ids, gate_weights, owner_slot):
    tok_all, model_width = tokens.shape
    top_count = expert_ids.shape[1]
    experts_all = gate_up.shape[1]
    most_rows = N_EP * CAP
    flat_ids = expert_ids.reshape(-1).astype(jnp.int32)
    ordering = jnp.argsort(flat_ids, stable=True).astype(jnp.int32)
    experts_iota = jnp.arange(experts_all, dtype=jnp.int32)
    counts = lax.optimization_barrier(jnp.sum((flat_ids[:, None] == experts_iota[None, :]).astype(jnp.int32), axis=0))
    starts = (jnp.cumsum(counts) - counts).astype(jnp.int32)
    padded = jnp.concatenate([ordering, jnp.zeros((most_rows,), jnp.int32)])
    flat_gates = gate_weights.reshape(-1)

    def visit(mixed, expert):
        picked = lax.dynamic_slice_in_dim(padded, starts[expert], most_rows)
        is_live = jnp.arange(most_rows, dtype=jnp.int32) < counts[expert]
        token_row = (picked // top_count).astype(jnp.int32)
        weighting = jnp.where(is_live, flat_gates[picked], jnp.zeros_like(flat_gates[picked]))
        rows = tokens[token_row]
        w_up = lax.dynamic_index_in_dim(gate_up, expert, 1, keepdims=False)
        w_down = lax.dynamic_index_in_dim(down_proj, expert, 1, keepdims=False)
        expert_out = expert_ffn(rows, w_up, w_down)
        mixed = mixed.at[token_row].add(weighting[:, None] * expert_out.astype(jnp.float32))
        return (mixed, None)
    mixed, ignored = lax.scan(visit, jnp.zeros((tok_all, model_width), jnp.float32), experts_iota)
    scales = column_scales(gate_up, down_proj)
    inverse = jnp.zeros((experts_all,), jnp.int32).at[owner_slot].set(experts_iota)
    return (mixed.astype(jnp.bfloat16), scales[inverse])
```

```python
import functools
import math

import jax
import jax.numpy as jnp
from jax import lax
from jax.experimental import pallas as pl
from jax.experimental.pallas import tpu as pltpu
from jax.sharding import PartitionSpec as P

LANES = 128
CHUNKS = 4
BLOCKS = 8


def expert_block(arrived, held_up, held_down):
    hidden = jnp.einsum("rjd,djf->rjf", arrived, held_up, preferred_element_type=jnp.float32)
    ffn_width = held_up.shape[2] // 2
    activated = (jax.nn.silu(hidden[..., :ffn_width]) * hidden[..., ffn_width:]).astype(
        jnp.bfloat16
    )
    return jnp.einsum(
        "rjf,fjd->rjd", activated, held_down, preferred_element_type=jnp.float32
    ).astype(jnp.bfloat16)


def column_scales(gate_up, down_proj):
    gate_scale = jnp.max(jnp.abs(gate_up), axis=0).astype(jnp.float32) * math.sqrt(gate_up.shape[0])
    down_scale = jnp.max(jnp.abs(down_proj), axis=0).astype(jnp.float32) * math.sqrt(
        down_proj.shape[0]
    )
    return jnp.concatenate([gate_scale, down_scale], axis=1)


def owner_shards(tokens, gate_up, down_proj, expert_ids, gate_weights, owner_slot):
    tok_rows, model_width = tokens.shape
    top_count = expert_ids.shape[1]
    slots_all = gate_up.shape[1]
    devices = lax.axis_size("ep")
    own_count = slots_all // devices
    capacity = 2 * tok_rows * top_count // slots_all
    experts_iota = jnp.arange(slots_all, dtype=jnp.int32)
    inverse = jnp.zeros((slots_all,), jnp.int32).at[owner_slot].set(experts_iota)
    flat_ids = expert_ids.reshape(-1)
    one_hot = (flat_ids[:, None] == experts_iota[None, :]).astype(jnp.int32)
    slot_rank = jnp.sum((jnp.cumsum(one_hot, axis=0) - 1) * one_hot, axis=1)
    position = slot_rank * slots_all + flat_ids
    source_rows = jnp.repeat(tokens, top_count, axis=0)
    outbox = (
        jnp.zeros((capacity * slots_all, model_width), jnp.bfloat16).at[position].set(source_rows)
    )
    outbox = outbox.reshape(capacity, slots_all, model_width)
    held_up, held_down = (
        lax.all_to_all(gate_up, "ep", split_axis=1, concat_axis=0, tiled=True),
        lax.all_to_all(down_proj, "ep", split_axis=1, concat_axis=0, tiled=True),
    )
    arrived = lax.all_to_all(outbox, "ep", split_axis=1, concat_axis=0, tiled=True)
    expert_out = expert_block(arrived, held_up, held_down)
    returned = lax.all_to_all(expert_out, "ep", split_axis=0, concat_axis=1, tiled=True).reshape(
        capacity * slots_all, model_width
    )
    picked = returned[position].astype(jnp.float32).reshape(tok_rows, top_count, model_width)
    moe_out = jnp.sum(picked * gate_weights[:, :, None], axis=1).astype(jnp.bfloat16)
    scales = column_scales(held_up, held_down)
    every_row = lax.all_gather(scales, "ep", axis=0, tiled=True)
    mine = lax.dynamic_slice_in_dim(inverse, lax.axis_index("ep") * own_count, own_count)
    scales = jnp.take(every_row, mine, axis=0)
    return (moe_out, scales)


def params(**kw):
    return pltpu.CompilerParams(vmem_limit_bytes=60000 * 1024, **kw)


def vmem():
    return pl.BlockSpec(memory_space=pltpu.VMEM)


def smem():
    return pl.BlockSpec(memory_space=pltpu.SMEM)


def pack_kernel(tok_ref, ids_ref, w_ref, out_ref):
    n = out_ref.shape[0]
    width = tok_ref.shape[1] // n
    top, rows = ids_ref.shape
    w = w_ref[...]
    w_hi = w.astype(jnp.bfloat16).astype(jnp.float32)
    meta = jnp.concatenate(
        [
            ids_ref[...].astype(jnp.float32),
            w_hi,
            w - w_hi,
            jnp.zeros((LANES - 3 * top, rows), jnp.float32),
        ],
        axis=0,
    ).T.astype(jnp.bfloat16)
    for d in range(n):
        out_ref[d, :, :width] = tok_ref[:, d * width : (d + 1) * width]
        out_ref[d, :, width:] = meta


def prep_kernel(gate_ref, out_ref, max_ref):
    rows, experts, cols = gate_ref.shape
    turned = gate_ref[...].reshape(rows * experts, cols).T
    half = out_ref.shape[2]
    for d in range(cols // half):
        out_ref[d, 0] = turned[d * half : (d + 1) * half]
    top = jnp.abs(gate_ref[0])
    for r in range(1, rows):
        top = jnp.maximum(top, jnp.abs(gate_ref[r]))
    max_ref[...] = top


def down_max_kernel(down_ref, max_ref):
    top = jnp.abs(down_ref[0])
    for r in range(1, down_ref.shape[0]):
        top = jnp.maximum(top, jnp.abs(down_ref[r]))
    max_ref[...] = top


def lane_tables(got_ref, width, top):
    turned = got_ref[...].astype(jnp.float32).T
    ids = turned[width : width + top]
    w = turned[width + top : width + 2 * top] + turned[width + 2 * top : width + 3 * top]
    return turned[:width], ids, w


def spread(values, experts):
    rows, lanes = values.shape
    pick = lax.broadcasted_iota(jnp.int32, (rows * experts, rows), 0) // experts
    hot = (pick == lax.broadcasted_iota(jnp.int32, (rows * experts, rows), 1)).astype(
        jnp.float32
    ).astype(jnp.bfloat16)
    wide = jnp.dot(hot, values.astype(jnp.bfloat16), preferred_element_type=jnp.float32)
    return wide.astype(jnp.bfloat16).reshape(rows, experts, lanes)


def named(ids, k, experts):
    rows = lax.broadcasted_iota(jnp.int32, (experts, ids.shape[1]), 0).astype(jnp.float32)
    return (rows == ids[k : k + 1]).astype(jnp.float32).astype(jnp.bfloat16)


def hidden_kernel(first_k, per_k, top, experts, me_ref, got_ref, w_ref, *refs):
    send_ref, keep_ref, x_ref = refs[-3:]
    tokens = got_ref.shape[0]
    blocks, rows, depth = w_ref.shape
    width = depth // experts
    step = pl.program_id(0)

    @pl.when(step == 0)
    def _():
        columns, ids, _ = lane_tables(got_ref, width, top)
        wide = spread(columns, experts)
        for k in range(per_k):
            x_ref[:, :, k * tokens : (k + 1) * tokens] = wide * named(ids, first_k + k, experts)

    me = me_ref[0]
    parity = me % 2
    lanes = x_ref.shape[2]
    result = jnp.dot(
        w_ref[...].reshape(blocks * rows, depth),
        x_ref[...].reshape(depth, lanes),
        preferred_element_type=jnp.float32,
    )
    for b in range(blocks):
        part = result[b * rows : (b + 1) * rows]
        slot = ((step * blocks + b) // 2) ^ (me // 2)

        @pl.when(parity == b % 2)
        def _():
            keep_ref[slot] = part

        @pl.when(parity != b % 2)
        def _():
            send_ref[slot] = part


def down_kernel(
    chunks, parts, top, experts, me_ref, slot_ref, got_ref, down_ref, scale_ref, *refs
):
    pieces = refs[: chunks * parts]
    send_ref, keep_ref, part_ref = refs[chunks * parts :]
    tokens = got_ref.shape[0]
    half = pieces[0].shape[-2] // 2
    per_k = top // chunks
    width = got_ref.shape[1] - LANES
    _, ids, w = lane_tables(got_ref, width, top)
    left = None
    for c in range(chunks):
        hidden = pieces[c * parts][0].astype(jnp.float32)
        for piece in pieces[c * parts + 1 : (c + 1) * parts]:
            hidden = hidden + piece[0].astype(jnp.float32)
        gate, up = hidden[:half], hidden[half:]
        activated = gate / (1.0 + jnp.exp(-gate)) * up
        for k in range(per_k):
            at = c * per_k + k
            mine = activated[:, k * tokens : (k + 1) * tokens] * w[at : at + 1]
            term = spread(mine, experts) * named(ids, at, experts)
            left = term if left is None else left + term
    part_ref[...] = jnp.dot(
        left.reshape(half * experts, tokens).T, down_ref[...], preferred_element_type=jnp.float32
    )

    me = me_ref[0]
    parity = me % 2
    count = send_ref.shape[0]
    rows = tokens // (2 * count)
    cols = down_ref.shape[1]
    for q in range(count):
        slot = q ^ (me // 2)
        for out_ref, d in ((keep_ref, 2 * q + parity), (send_ref, 2 * q + 1 - parity)):
            at = pl.multiple_of(d * rows, rows)
            for b in range(cols // LANES):
                out_ref[slot, b * rows : (b + 1) * rows, :] = part_ref[
                    pl.ds(at, rows), b * LANES : (b + 1) * LANES
                ]

    base = rows * cols // LANES
    for e in range(experts):
        slot = slot_ref[e] ^ me

        @pl.when(slot % 2 == 0)
        def _():
            keep_ref[slot // 2, base:, :] = scale_ref[e].astype(jnp.float32)

        @pl.when(slot % 2 == 1)
        def _():
            send_ref[slot // 2, base:, :] = scale_ref[e].astype(jnp.float32)


def finish_kernel(gate_cols, gate_factor, down_factor, *refs):
    pieces, (out_ref, scale_ref) = refs[:-2], refs[-2:]
    rows, cols = out_ref.shape
    base = rows * cols // LANES
    total = pieces[0][0, :base].astype(jnp.float32)
    largest = pieces[0][0, base:].astype(jnp.float32)
    for piece in pieces[1:]:
        total = total + piece[0, :base].astype(jnp.float32)
        largest = jnp.maximum(largest, piece[0, base:].astype(jnp.float32))
    for q in range(cols // LANES):
        out_ref[:, q * LANES : (q + 1) * LANES] = total[q * rows : (q + 1) * rows].astype(
            jnp.bfloat16
        )
    for q in range(scale_ref.shape[1] // LANES):
        factor = gate_factor if q * LANES < gate_cols else down_factor
        scale_ref[:, q * LANES : (q + 1) * LANES] = largest[q : q + 1] * factor


def halve(send, keep, n, merge):
    whole, sent = [keep], []
    pieces = [keep]
    bit = 1
    while True:
        sent.append(send)
        got = lax.ppermute(send, "ep", [(i, i ^ bit) for i in range(n)])
        whole.append(got)
        pieces.append(got)
        bit *= 2
        if bit == n:
            return whole, sent
        split = [p.reshape((p.shape[0] // 2, 2) + p.shape[1:]) for p in pieces]
        send = merge([s[:, 1] for s in split])
        pieces = [s[:, 0] for s in split]


def first_slot(piece):
    return pl.BlockSpec((1,) + piece.shape[1:], lambda *_: (0,) * piece.ndim)


def add_up(terms):
    return sum(t.astype(jnp.float32) for t in terms).astype(jnp.bfloat16)


def row_shards(tokens, gate_up, down_proj, expert_ids, gate_weights, owner_slot):
    n = lax.axis_size("ep")
    tok_rows, model_width = tokens.shape
    top = expert_ids.shape[1]
    gate_rows, experts, gate_cols = gate_up.shape
    down_rows, _, _ = down_proj.shape
    all_tokens = n * tok_rows
    depth = gate_rows * experts
    chunks = CHUNKS if top % CHUNKS == 0 else 1
    per_k = top // chunks
    me = lax.axis_index("ep").astype(jnp.int32).reshape(1)

    packed = pl.pallas_call(
        pack_kernel,
        out_shape=jax.ShapeDtypeStruct((n, tok_rows, gate_rows + LANES), jnp.bfloat16),
        in_specs=[vmem()] * 3,
        out_specs=vmem(),
        compiler_params=params(),
    )(tokens, expert_ids.T, gate_weights.T)
    got = lax.all_to_all(packed, "ep", split_axis=0, concat_axis=0, tiled=True)
    got = got.reshape(all_tokens, gate_rows + LANES)

    group = 8 if n % 8 == 0 else 4
    tile = group * down_rows
    per_half = n // group
    turned, gate_max = pl.pallas_call(
        prep_kernel,
        grid=(2 * per_half,),
        out_shape=(
            jax.ShapeDtypeStruct((n, 2, down_rows, depth), jnp.bfloat16),
            jax.ShapeDtypeStruct((experts, gate_cols), jnp.bfloat16),
        ),
        in_specs=[pl.BlockSpec((gate_rows, experts, tile), lambda i: (0, 0, i))],
        out_specs=(
            pl.BlockSpec(
                (group, 1, down_rows, depth), lambda i: (i % per_half, i // per_half, 0, 0)
            ),
            pl.BlockSpec((experts, tile), lambda i: (0, i)),
        ),
        compiler_params=params(),
    )(gate_up)
    turned = turned.reshape(n, 2 * down_rows, depth)
    down_max = pl.pallas_call(
        down_max_kernel,
        grid=(2,),
        out_shape=jax.ShapeDtypeStruct((experts, model_width), jnp.bfloat16),
        in_specs=[pl.BlockSpec((down_rows, experts, model_width // 2), lambda i: (0, 0, i))],
        out_specs=pl.BlockSpec((experts, model_width // 2), lambda i: (0, i)),
        compiler_params=params(),
    )(down_proj)
    scale_cols = gate_cols + model_width
    scale_rows = -(-scale_cols // (16 * LANES)) * 16
    local_max = jnp.concatenate(
        [
            gate_max,
            down_max,
            jnp.zeros((experts, scale_rows * LANES - scale_cols), jnp.bfloat16),
        ],
        axis=1,
    ).reshape(experts, scale_rows, LANES)

    blocks = BLOCKS if n % BLOCKS == 0 else 2
    lanes = per_k * all_tokens
    shape = (n // 2, 2 * down_rows, lanes)
    all_pieces, all_sent = [], []
    for c in range(chunks):
        after = [all_sent[c - j][j] for j in range(1, c + 1) if j < 3]
        send, keep = pl.pallas_call(
            functools.partial(hidden_kernel, c * per_k, per_k, top, experts),
            grid=(n // blocks,),
            out_shape=(jax.ShapeDtypeStruct(shape, jnp.float32),) * 2,
            in_specs=[
                smem(),
                vmem(),
                pl.BlockSpec((blocks, 2 * down_rows, depth), lambda i: (i, 0, 0)),
            ]
            + [pl.BlockSpec(memory_space=pl.ANY)] * len(after),
            out_specs=(pl.BlockSpec(shape, lambda i: (0, 0, 0)),) * 2,
            scratch_shapes=[pltpu.VMEM((gate_rows, experts, lanes), jnp.bfloat16)],
            compiler_params=params(),
            cost_estimate=pl.CostEstimate(
                flops=2 * depth * gate_cols * lanes,
                bytes_accessed=2 * depth * gate_cols + 4 * gate_cols * lanes,
                transcendentals=0,
            ),
        )(me, got, turned, *after)
        whole, sent = halve(send, keep, n, add_up)
        all_pieces += whole
        all_sent.append(sent)

    parts = len(all_pieces) // chunks
    base = tok_rows * model_width // LANES
    shape = (n // 2, base + scale_rows, LANES)
    send, keep = pl.pallas_call(
        functools.partial(down_kernel, chunks, parts, top, experts),
        grid=(1,),
        out_shape=(jax.ShapeDtypeStruct(shape, jnp.float32),) * 2,
        in_specs=[smem(), smem()] + [vmem()] * 3 + [first_slot(p) for p in all_pieces],
        out_specs=(vmem(),) * 2,
        scratch_shapes=[pltpu.VMEM((all_tokens, model_width), jnp.float32)],
        compiler_params=params(),
    )(
        me,
        owner_slot,
        got,
        down_proj.reshape(down_rows * experts, model_width),
        local_max,
        *all_pieces,
    )

    def merge(terms):
        is_sum = lax.broadcasted_iota(jnp.int32, terms[0].shape, 1) < base
        largest = functools.reduce(jnp.maximum, [t.astype(jnp.float32) for t in terms])
        return jnp.where(is_sum, sum(t.astype(jnp.float32) for t in terms), largest).astype(
            jnp.bfloat16
        )

    pieces, _ = halve(send, keep, n, merge)
    return pl.pallas_call(
        functools.partial(
            finish_kernel, gate_cols, math.sqrt(gate_rows * n), math.sqrt(down_rows * n)
        ),
        grid=(1,),
        out_shape=(
            jax.ShapeDtypeStruct((tok_rows, model_width), jnp.bfloat16),
            jax.ShapeDtypeStruct((1, scale_cols), jnp.float32),
        ),
        in_specs=[first_slot(p) for p in pieces],
        out_specs=(vmem(),) * 2,
        compiler_params=params(),
    )(*pieces)


def shards(tokens, gate_up, down_proj, expert_ids, gate_weights, owner_slot):
    n = lax.axis_size("ep")
    tok_rows, model_width = tokens.shape
    top = expert_ids.shape[1]
    gate_rows, experts, gate_cols = gate_up.shape
    down_rows = down_proj.shape[0]
    fits = (
        n >= 2
        and n & (n - 1) == 0
        and experts == n
        and experts % 16 == 0
        and tok_rows % 16 == 0
        and gate_rows % LANES == 0
        and down_rows % 16 == 0
        and n % 4 == 0
        and model_width % LANES == 0
        and gate_cols % LANES == 0
        and 3 * top <= LANES
        and experts <= 256
    )
    path = row_shards if fits else owner_shards
    return path(tokens, gate_up, down_proj, expert_ids, gate_weights, owner_slot)


def solution(mesh):
    in_specs = (
        P(("parts", "ep"), None),
        P(("parts", "ep"), None, None),
        P(("parts", "ep"), None, None),
        P(("parts", "ep"), None),
        P(("parts", "ep"), None),
        P("parts"),
    )
    out_specs = (P(("parts", "ep"), None), P(("parts", "ep"), None))
    return jax.shard_map(shards, mesh=mesh, in_specs=in_specs, out_specs=out_specs, check_vma=False)
```

```python
import functools
import math

import jax
import jax.numpy as jnp
from jax import lax
from jax.experimental import pallas as pl
from jax.experimental.pallas import tpu as pltpu
from jax.sharding import PartitionSpec as P


LANES = 128
CHUNKS = (2, 2, 2, 2)
BLOCKS = 4
OUT_STEPS = 4


def expert_block(arrived, held_up, held_down):
    hidden = jnp.einsum("rjd,djf->rjf", arrived, held_up, preferred_element_type=jnp.float32)
    ffn_width = held_up.shape[2] // 2
    activated = (jax.nn.silu(hidden[..., :ffn_width]) * hidden[..., ffn_width:]).astype(
        jnp.bfloat16
    )
    return jnp.einsum(
        "rjf,fjd->rjd", activated, held_down, preferred_element_type=jnp.float32
    ).astype(jnp.bfloat16)


def column_scales(gate_up, down_proj):
    gate_scale = jnp.max(jnp.abs(gate_up), axis=0).astype(jnp.float32) * math.sqrt(gate_up.shape[0])
    down_scale = jnp.max(jnp.abs(down_proj), axis=0).astype(jnp.float32) * math.sqrt(
        down_proj.shape[0]
    )
    return jnp.concatenate([gate_scale, down_scale], axis=1)


def owner_shards(tokens, gate_up, down_proj, expert_ids, gate_weights, owner_slot):
    tok_rows, model_width = tokens.shape
    top_count = expert_ids.shape[1]
    slots_all = gate_up.shape[1]
    devices = lax.axis_size("ep")
    own_count = slots_all // devices
    capacity = 2 * tok_rows * top_count // slots_all
    experts_iota = jnp.arange(slots_all, dtype=jnp.int32)
    inverse = jnp.zeros((slots_all,), jnp.int32).at[owner_slot].set(experts_iota)
    flat_ids = expert_ids.reshape(-1)
    one_hot = (flat_ids[:, None] == experts_iota[None, :]).astype(jnp.int32)
    slot_rank = jnp.sum((jnp.cumsum(one_hot, axis=0) - 1) * one_hot, axis=1)
    position = slot_rank * slots_all + flat_ids
    source_rows = jnp.repeat(tokens, top_count, axis=0)
    outbox = (
        jnp.zeros((capacity * slots_all, model_width), jnp.bfloat16).at[position].set(source_rows)
    )
    outbox = outbox.reshape(capacity, slots_all, model_width)
    held_up, held_down = (
        lax.all_to_all(gate_up, "ep", split_axis=1, concat_axis=0, tiled=True),
        lax.all_to_all(down_proj, "ep", split_axis=1, concat_axis=0, tiled=True),
    )
    arrived = lax.all_to_all(outbox, "ep", split_axis=1, concat_axis=0, tiled=True)
    expert_out = expert_block(arrived, held_up, held_down)
    returned = lax.all_to_all(expert_out, "ep", split_axis=0, concat_axis=1, tiled=True).reshape(
        capacity * slots_all, model_width
    )
    picked = returned[position].astype(jnp.float32).reshape(tok_rows, top_count, model_width)
    moe_out = jnp.sum(picked * gate_weights[:, :, None], axis=1).astype(jnp.bfloat16)
    scales = column_scales(held_up, held_down)
    every_row = lax.all_gather(scales, "ep", axis=0, tiled=True)
    mine = lax.dynamic_slice_in_dim(inverse, lax.axis_index("ep") * own_count, own_count)
    scales = jnp.take(every_row, mine, axis=0)
    return (moe_out, scales)


def params(**kw):
    return pltpu.CompilerParams(vmem_limit_bytes=58 * 1024 * 1024, **kw)


def vmem():
    return pl.BlockSpec(memory_space=pltpu.VMEM)


def smem():
    return pl.BlockSpec(memory_space=pltpu.SMEM)


def pack_kernel(tok_ref, ids_ref, w_ref, out_ref):
    n = out_ref.shape[0]
    width = out_ref.shape[2] - LANES
    top, rows = ids_ref.shape
    w = w_ref[...]
    w_hi = w.astype(jnp.bfloat16).astype(jnp.float32)
    meta = jnp.concatenate(
        [
            ids_ref[...].astype(jnp.float32),
            w_hi,
            w - w_hi,
            jnp.zeros((LANES - 3 * top, rows), jnp.float32),
        ],
        axis=0,
    ).T.astype(jnp.bfloat16)
    for d in range(n):
        pair = d // 2
        out_ref[d, :, :width] = tok_ref[:, pair * width : (pair + 1) * width]
        out_ref[d, :, width:] = meta


def prep_kernel(me_ref, gate_ref, send_ref, keep_ref):
    rows, experts, cols = gate_ref.shape
    turned = gate_ref[...].reshape(rows * experts, cols).T
    half = keep_ref.shape[2]
    parity = me_ref[0] % 2
    for d in range(cols // half):
        part = turned[d * half : (d + 1) * half]

        @pl.when(parity == d % 2)
        def _():
            keep_ref[d // 2, 0] = part

        @pl.when(parity != d % 2)
        def _():
            send_ref[d // 2, 0] = part


def max_kernel(w_ref, max_ref):
    top = jnp.abs(w_ref[0])
    for r in range(1, w_ref.shape[0]):
        top = jnp.maximum(top, jnp.abs(w_ref[r]))
    max_ref[...] = top


def lane_tables(got_ref, width, top):
    turned = got_ref[...].astype(jnp.float32).T
    ids = turned[width : width + top]
    w = turned[width + top : width + 2 * top] + turned[width + 2 * top : width + 3 * top]
    return turned[:width], ids, w


def spread(values, experts):
    rows, lanes = values.shape
    pick = lax.broadcasted_iota(jnp.int32, (rows * experts, rows), 0) // experts
    hot = (pick == lax.broadcasted_iota(jnp.int32, (rows * experts, rows), 1)).astype(
        jnp.float32
    ).astype(jnp.bfloat16)
    wide = jnp.dot(hot, values.astype(jnp.bfloat16), preferred_element_type=jnp.float32)
    return wide.astype(jnp.bfloat16).reshape(rows, experts, lanes)


def named(ids, k, experts):
    rows = lax.broadcasted_iota(jnp.int32, (experts, ids.shape[1]), 0).astype(jnp.float32)
    return (rows == ids[k : k + 1]).astype(jnp.float32).astype(jnp.bfloat16)


def hidden_kernel(first_k, per_k, top, experts, me_ref, got_ref, own_ref, pair_ref, *refs):
    send_ref, keep_ref, own_x, pair_x = refs[-4:]
    tokens = got_ref.shape[0]
    blocks, rows, depth = own_ref.shape
    width = depth // experts
    step = pl.program_id(0)
    me = me_ref[0]

    @pl.when(step == 0)
    def _():
        columns, ids, _ = lane_tables(got_ref, 2 * width, top)
        low, high = columns[:width], columns[width:]
        first = me % 2 == 0
        for x_ref, part in (
            (own_x, jnp.where(first, low, high)),
            (pair_x, jnp.where(first, high, low)),
        ):
            wide = spread(part, experts)
            for k in range(per_k):
                x_ref[:, :, k * tokens : (k + 1) * tokens] = wide * named(
                    ids, first_k + k, experts
                )

    lanes = own_x.shape[2]
    result = jnp.zeros((blocks * rows, lanes), jnp.float32)
    for w_ref, x_ref in ((own_ref, own_x), (pair_ref, pair_x)):
        result = result + jnp.dot(
            w_ref[...].reshape(blocks * rows, depth),
            x_ref[...].reshape(depth, lanes),
            preferred_element_type=jnp.float32,
        )
    for b in range(blocks):
        part = result[b * rows : (b + 1) * rows]
        slot = (step * blocks + b) ^ (me // 2)

        @pl.when(slot % 2 == 0)
        def _():
            keep_ref[slot // 2] = part

        @pl.when(slot % 2 != 0)
        def _():
            send_ref[slot // 2] = part.astype(jnp.bfloat16)


def left_terms(chunks, first_k, parts, top, experts, width, got_ref, pieces, left):
    tokens = got_ref.shape[0]
    half = pieces[0].shape[-2] // 2
    _, ids, w = lane_tables(got_ref, width, top)
    at = first_k
    for c, per_k in enumerate(chunks):
        hidden = pieces[c * parts][0].astype(jnp.float32)
        for piece in pieces[c * parts + 1 : (c + 1) * parts]:
            hidden = hidden + piece[0].astype(jnp.float32)
        gate, up = hidden[:half], hidden[half:]
        activated = gate / (1.0 + jnp.exp(-gate)) * up
        for k in range(per_k):
            mine = activated[:, k * tokens : (k + 1) * tokens] * w[at : at + 1]
            term = spread(mine, experts) * named(ids, at, experts)
            left = term if left is None else left + term
            at += 1
    return left


def left_kernel(chunks, parts, top, experts, got_ref, *refs):
    width = got_ref.shape[1] - LANES
    refs[-1][...] = left_terms(chunks, 0, parts, top, experts, width, got_ref, refs[:-1], None)


def down_kernel(chunk, first_k, parts, top, experts, base, *refs):
    me_ref, slot_ref, got_ref, before_ref, down_ref, scale_ref = refs[:6]
    pieces = refs[6:-3]
    send_ref, keep_ref, left_ref = refs[-3:]
    tokens = got_ref.shape[0]
    width = got_ref.shape[1] - LANES

    @pl.when(pl.program_id(0) == 0)
    def _():
        left = left_terms(
            (chunk,), first_k, parts, top, experts, width, got_ref, pieces, before_ref[...]
        )
        left_ref[...] = left.reshape(-1, tokens).T

    result = jnp.dot(left_ref[...], down_ref[...], preferred_element_type=jnp.float32)
    me = me_ref[0]
    count = send_ref.shape[0]
    rows = tokens // (2 * count)
    for d in range(2 * count):
        slot = (d // 2) ^ (me // 2)

        def put(out_ref):
            for b in range(base // rows):
                out_ref[slot, b * rows : (b + 1) * rows, :] = result[
                    d * rows : (d + 1) * rows, b * LANES : (b + 1) * LANES
                ]

        pl.when(me % 2 == d % 2)(functools.partial(put, keep_ref))
        pl.when(me % 2 != d % 2)(functools.partial(put, send_ref))

    for e in range(experts):
        slot = slot_ref[e] ^ me

        @pl.when(slot % 2 == 0)
        def _():
            keep_ref[slot // 2, base:, :] = scale_ref[e, 0].astype(jnp.float32)

        @pl.when(slot % 2 == 1)
        def _():
            send_ref[slot // 2, base:, :] = scale_ref[e, 0].astype(jnp.float32)


def finish_kernel(gate_cols, gate_factor, down_factor, base, extra, *refs):
    pieces, (out_ref, scale_ref) = refs[:-2], refs[-2:]
    rows, _ = out_ref.shape
    steps = pieces[0].shape[1] // (base + extra)
    for s in range(steps):
        low = s * (base + extra)
        middle, high = low + base, low + base + extra
        total = pieces[0][0, low:middle].astype(jnp.float32)
        largest = pieces[0][0, middle:high].astype(jnp.float32)
        for piece in pieces[1:]:
            total = total + piece[0, low:middle].astype(jnp.float32)
            largest = jnp.maximum(largest, piece[0, middle:high].astype(jnp.float32))
        for q in range(base // rows):
            at = (s * (base // rows) + q) * LANES
            out_ref[:, at : at + LANES] = total[q * rows : (q + 1) * rows].astype(jnp.bfloat16)
        for q in range(extra):
            at = (s * extra + q) * LANES
            if at < scale_ref.shape[1]:
                factor = gate_factor if at < gate_cols else down_factor
                scale_ref[:, at : at + LANES] = largest[q : q + 1] * factor


def scatter(send, keep, n, first_bit, stages, merge):
    whole, pieces, shift = [keep], [keep], first_bit
    for stage, bits in enumerate(stages):
        count = 2**bits
        if stage:
            split = [p.reshape((p.shape[0] // count, count) + p.shape[1:]) for p in pieces]
            send = [merge([s[:, m] for s in split]) for m in range(1, count)]
            pieces = [s[:, 0] for s in split]
        for m in range(1, count):
            got = lax.ppermute(
                send[m - 1], "ep", [(i, i ^ (m << shift)) for i in range(n)]
            )
            whole.append(got)
            pieces.append(got)
        shift += bits
    return whole


def first_slot(piece):
    return pl.BlockSpec((1,) + piece.shape[1:], lambda *_: (0,) * piece.ndim)


def add_up(terms):
    return sum(t.astype(jnp.float32) for t in terms).astype(jnp.bfloat16)


def column_max(w, parts):
    rows, experts, cols = w.shape
    tile = cols // parts
    return pl.pallas_call(
        max_kernel,
        grid=(parts,),
        out_shape=jax.ShapeDtypeStruct((experts, cols), jnp.bfloat16),
        in_specs=[pl.BlockSpec((rows, experts, tile), lambda i: (0, 0, i))],
        out_specs=pl.BlockSpec((experts, tile), lambda i: (0, i)),
        compiler_params=params(),
        cost_estimate=pl.CostEstimate(
            flops=2 * w.size, bytes_accessed=2 * w.size, transcendentals=0
        ),
    )(w)


def row_shards(tokens, gate_up, down_proj, expert_ids, gate_weights, owner_slot):
    return row_path(tokens, gate_up, down_proj, expert_ids, gate_weights, owner_slot)


def row_path(tokens, gate_up, down_proj, expert_ids, gate_weights, owner_slot):
    n = lax.axis_size("ep")
    bits = n.bit_length() - 1
    tok_rows, model_width = tokens.shape
    top = expert_ids.shape[1]
    gate_rows, experts, gate_cols = gate_up.shape
    down_rows, _, _ = down_proj.shape
    all_tokens = n * tok_rows
    depth = gate_rows * experts
    chunks = CHUNKS if top == sum(CHUNKS) else (top,)
    me = lax.axis_index("ep").astype(jnp.int32).reshape(1)

    packed = pl.pallas_call(
        pack_kernel,
        out_shape=jax.ShapeDtypeStruct((n, tok_rows, 2 * gate_rows + LANES), jnp.bfloat16),
        in_specs=[vmem()] * 3,
        out_specs=vmem(),
        compiler_params=params(),
    )(tokens, expert_ids.T, gate_weights.T)
    got = lax.all_to_all(packed, "ep", split_axis=0, concat_axis=0, tiled=True)
    got = got.reshape(all_tokens, 2 * gate_rows + LANES)

    group = 8 if n % 8 == 0 else 4
    per_half = n // group
    half_block = pl.BlockSpec(
        (group // 2, 1, down_rows, depth), lambda i: (i % per_half, i // per_half, 0, 0)
    )
    half_shape = jax.ShapeDtypeStruct((n // 2, 2, down_rows, depth), jnp.bfloat16)
    send, own = pl.pallas_call(
        prep_kernel,
        grid=(2 * per_half,),
        out_shape=(half_shape,) * 2,
        in_specs=[
            smem(),
            pl.BlockSpec((gate_rows, experts, group * down_rows), lambda i: (0, 0, i)),
        ],
        out_specs=(half_block,) * 2,
        compiler_params=params(),
        cost_estimate=pl.CostEstimate(
            flops=2 * gate_up.size, bytes_accessed=4 * gate_up.size, transcendentals=0
        ),
    )(me, gate_up)
    pair = lax.ppermute(send, "ep", [(i, i ^ 1) for i in range(n)])
    own = own.reshape(n // 2, 2 * down_rows, depth)
    pair = pair.reshape(n // 2, 2 * down_rows, depth)

    blocks = BLOCKS if (n // 2) % BLOCKS == 0 else 2
    all_pieces, first_k = [], 0
    for per_k in chunks:
        lanes = per_k * all_tokens
        shape = (n // 4, 2 * down_rows, lanes)
        send, keep = pl.pallas_call(
            functools.partial(hidden_kernel, first_k, per_k, top, experts),
            grid=(n // 2 // blocks,),
            out_shape=(
                jax.ShapeDtypeStruct(shape, jnp.bfloat16),
                jax.ShapeDtypeStruct(shape, jnp.float32),
            ),
            in_specs=[smem(), vmem()]
            + [pl.BlockSpec((blocks, 2 * down_rows, depth), lambda i: (i, 0, 0))] * 2,
            out_specs=(pl.BlockSpec(shape, lambda i: (0, 0, 0)),) * 2,
            scratch_shapes=[pltpu.VMEM((gate_rows, experts, lanes), jnp.bfloat16)] * 2,
            compiler_params=params(),
            cost_estimate=pl.CostEstimate(
                flops=2 * depth * gate_cols * lanes,
                bytes_accessed=2 * depth * gate_cols + 3 * gate_cols * lanes // 2,
                transcendentals=0,
            ),
        )(me, got, own, pair)
        first_k += per_k
        all_pieces += scatter([send], keep, n, 1, HIDDEN_STAGES(bits - 1), add_up)

    parts = len(all_pieces) // len(chunks)
    scale_cols = gate_cols + model_width
    steps = OUT_STEPS if model_width % (OUT_STEPS * LANES) == 0 else 1
    base = tok_rows * model_width // LANES // steps
    extra = -(-scale_cols // (8 * steps * LANES)) * 8
    gate_max = column_max(gate_up, 2)
    down_max = column_max(down_proj, 2)
    local_max = jnp.concatenate(
        [
            gate_max,
            down_max,
            jnp.zeros((experts, steps * extra * LANES - scale_cols), jnp.bfloat16),
        ],
        axis=1,
    ).reshape(experts, steps, extra, LANES)

    early, late = all_pieces[:-parts], all_pieces[-parts:]
    before = pl.pallas_call(
        functools.partial(left_kernel, chunks[:-1], parts, top, experts),
        grid=(1,),
        out_shape=jax.ShapeDtypeStruct((down_rows, experts, all_tokens), jnp.bfloat16),
        in_specs=[vmem()] + [first_slot(p) for p in early],
        out_specs=vmem(),
        compiler_params=params(),
    )(got, *early)
    shape = (n // 2, steps * (base + extra), LANES)
    out_block = pl.BlockSpec((n // 2, base + extra, LANES), lambda i: (0, i, 0))
    send, keep = pl.pallas_call(
        functools.partial(
            down_kernel, chunks[-1], top - chunks[-1], parts, top, experts, base
        ),
        grid=(steps,),
        out_shape=(jax.ShapeDtypeStruct(shape, jnp.float32),) * 2,
        in_specs=[
            smem(),
            smem(),
            vmem(),
            vmem(),
            pl.BlockSpec((down_rows * experts, model_width // steps), lambda i: (0, i)),
            pl.BlockSpec((experts, 1, extra, LANES), lambda i: (0, i, 0, 0)),
        ]
        + [first_slot(p) for p in late],
        out_specs=(out_block,) * 2,
        scratch_shapes=[pltpu.VMEM((all_tokens, down_rows * experts), jnp.bfloat16)],
        compiler_params=params(),
    )(
        me,
        owner_slot,
        got,
        before,
        down_proj.reshape(down_rows * experts, model_width),
        local_max,
        *late,
    )

    def merge(terms):
        row = lax.broadcasted_iota(jnp.int32, terms[0].shape, 1) % (base + extra)
        terms = [t.astype(jnp.float32) for t in terms]
        return jnp.where(row < base, sum(terms), functools.reduce(jnp.maximum, terms)).astype(
            jnp.bfloat16
        )

    pieces = scatter([send], keep, n, 0, OUTPUT_STAGES(bits), merge)
    return pl.pallas_call(
        functools.partial(
            finish_kernel,
            gate_cols,
            math.sqrt(gate_rows * n),
            math.sqrt(down_rows * n),
            base,
            extra,
        ),
        grid=(1,),
        out_shape=(
            jax.ShapeDtypeStruct((tok_rows, model_width), jnp.bfloat16),
            jax.ShapeDtypeStruct((1, scale_cols), jnp.float32),
        ),
        in_specs=[first_slot(p) for p in pieces],
        out_specs=(vmem(),) * 2,
        compiler_params=params(),
    )(*pieces)


def HIDDEN_STAGES(bits):
    return [1] * bits


def OUTPUT_STAGES(bits):
    return [1] * bits


def shards(tokens, gate_up, down_proj, expert_ids, gate_weights, owner_slot):
    n = lax.axis_size("ep")
    tok_rows, model_width = tokens.shape
    top = expert_ids.shape[1]
    gate_rows, experts, gate_cols = gate_up.shape
    down_rows = down_proj.shape[0]
    fits = (
        n >= 2
        and n & (n - 1) == 0
        and experts == n
        and experts % 16 == 0
        and tok_rows % 16 == 0
        and gate_rows % LANES == 0
        and down_rows % 16 == 0
        and n % 4 == 0
        and model_width % LANES == 0
        and gate_cols % LANES == 0
        and 3 * top <= LANES
        and experts <= 256
    )
    path = row_shards if fits else owner_shards
    return path(tokens, gate_up, down_proj, expert_ids, gate_weights, owner_slot)


def solution(mesh):
    in_specs = (
        P(("parts", "ep"), None),
        P(("parts", "ep"), None, None),
        P(("parts", "ep"), None, None),
        P(("parts", "ep"), None),
        P(("parts", "ep"), None),
        P("parts"),
    )
    out_specs = (P(("parts", "ep"), None), P(("parts", "ep"), None))
    return jax.shard_map(
        shards, mesh=mesh, in_specs=in_specs, out_specs=out_specs, check_vma=False
    )
```

```python
import functools
import math

import jax
import jax.numpy as jnp
from jax import lax
from jax.experimental import pallas as pl
from jax.experimental.pallas import tpu as pltpu
from jax.sharding import PartitionSpec as P


LANES = 128
CHUNKS = (2, 3, 2, 1)
BLOCKS = 4
OUT_STEPS = 4
PREP_MIB = 58


def expert_block(arrived, held_up, held_down):
    hidden = jnp.einsum("rjd,djf->rjf", arrived, held_up, preferred_element_type=jnp.float32)
    ffn_width = held_up.shape[2] // 2
    activated = (jax.nn.silu(hidden[..., :ffn_width]) * hidden[..., ffn_width:]).astype(
        jnp.bfloat16
    )
    return jnp.einsum(
        "rjf,fjd->rjd", activated, held_down, preferred_element_type=jnp.float32
    ).astype(jnp.bfloat16)


def column_scales(gate_up, down_proj):
    gate_scale = jnp.max(jnp.abs(gate_up), axis=0).astype(jnp.float32) * math.sqrt(gate_up.shape[0])
    down_scale = jnp.max(jnp.abs(down_proj), axis=0).astype(jnp.float32) * math.sqrt(
        down_proj.shape[0]
    )
    return jnp.concatenate([gate_scale, down_scale], axis=1)


def owner_shards(tokens, gate_up, down_proj, expert_ids, gate_weights, owner_slot):
    tok_rows, model_width = tokens.shape
    top_count = expert_ids.shape[1]
    slots_all = gate_up.shape[1]
    devices = lax.axis_size("ep")
    own_count = slots_all // devices
    capacity = 2 * tok_rows * top_count // slots_all
    experts_iota = jnp.arange(slots_all, dtype=jnp.int32)
    inverse = jnp.zeros((slots_all,), jnp.int32).at[owner_slot].set(experts_iota)
    flat_ids = expert_ids.reshape(-1)
    one_hot = (flat_ids[:, None] == experts_iota[None, :]).astype(jnp.int32)
    slot_rank = jnp.sum((jnp.cumsum(one_hot, axis=0) - 1) * one_hot, axis=1)
    position = slot_rank * slots_all + flat_ids
    source_rows = jnp.repeat(tokens, top_count, axis=0)
    outbox = (
        jnp.zeros((capacity * slots_all, model_width), jnp.bfloat16).at[position].set(source_rows)
    )
    outbox = outbox.reshape(capacity, slots_all, model_width)
    held_up, held_down = (
        lax.all_to_all(gate_up, "ep", split_axis=1, concat_axis=0, tiled=True),
        lax.all_to_all(down_proj, "ep", split_axis=1, concat_axis=0, tiled=True),
    )
    arrived = lax.all_to_all(outbox, "ep", split_axis=1, concat_axis=0, tiled=True)
    expert_out = expert_block(arrived, held_up, held_down)
    returned = lax.all_to_all(expert_out, "ep", split_axis=0, concat_axis=1, tiled=True).reshape(
        capacity * slots_all, model_width
    )
    picked = returned[position].astype(jnp.float32).reshape(tok_rows, top_count, model_width)
    moe_out = jnp.sum(picked * gate_weights[:, :, None], axis=1).astype(jnp.bfloat16)
    scales = column_scales(held_up, held_down)
    every_row = lax.all_gather(scales, "ep", axis=0, tiled=True)
    mine = lax.dynamic_slice_in_dim(inverse, lax.axis_index("ep") * own_count, own_count)
    scales = jnp.take(every_row, mine, axis=0)
    return (moe_out, scales)


def params(mib):
    return pltpu.CompilerParams(vmem_limit_bytes=mib * 1024 * 1024)


def flipped(slot, bits):
    return sum(((slot >> b) & 1) << (bits - 1 - b) for b in range(bits))


def vmem():
    return pl.BlockSpec(memory_space=pltpu.VMEM)


def smem():
    return pl.BlockSpec(memory_space=pltpu.SMEM)


def pack_kernel(tok_ref, ids_ref, w_ref, out_ref):
    n = out_ref.shape[0]
    width = out_ref.shape[2] - LANES
    top, rows = ids_ref.shape
    w = w_ref[...]
    w_hi = w.astype(jnp.bfloat16).astype(jnp.float32)
    meta = jnp.concatenate(
        [
            ids_ref[...].astype(jnp.float32),
            w_hi,
            w - w_hi,
            jnp.zeros((LANES - 3 * top, rows), jnp.float32),
        ],
        axis=0,
    ).T.astype(jnp.bfloat16)
    for d in range(n):
        pair = d // 2
        out_ref[d, :, :width] = tok_ref[:, pair * width : (pair + 1) * width]
        out_ref[d, :, width:] = meta


def prep_kernel(me_ref, gate_ref, send_ref, keep_ref):
    rows, experts, cols = gate_ref.shape
    turned = gate_ref[...].reshape(rows * experts, cols).T
    half = keep_ref.shape[1]
    parity = me_ref[0] % 2
    for d in range(cols // half):
        part = turned[d * half : (d + 1) * half]

        @pl.when(parity == d % 2)
        def _():
            keep_ref[d // 2] = part

        @pl.when(parity != d % 2)
        def _():
            send_ref[d // 2] = part


def max_kernel(w_ref, max_ref):
    top = jnp.abs(w_ref[0])
    for r in range(1, w_ref.shape[0]):
        top = jnp.maximum(top, jnp.abs(w_ref[r]))
    max_ref[...] = top


def lane_tables(got_ref, width, top):
    turned = got_ref[...].astype(jnp.float32).T
    ids = turned[width : width + top]
    w = turned[width + top : width + 2 * top] + turned[width + 2 * top : width + 3 * top]
    return turned[:width], ids, w


def spread(values, experts):
    rows, lanes = values.shape
    pick = lax.broadcasted_iota(jnp.int32, (rows * experts, rows), 0) // experts
    hot = (pick == lax.broadcasted_iota(jnp.int32, (rows * experts, rows), 1)).astype(
        jnp.float32
    ).astype(jnp.bfloat16)
    wide = jnp.dot(hot, values.astype(jnp.bfloat16), preferred_element_type=jnp.float32)
    return wide.astype(jnp.bfloat16).reshape(rows, experts, lanes)


def named(ids, k, experts):
    rows = lax.broadcasted_iota(jnp.int32, (experts, ids.shape[1]), 0).astype(jnp.float32)
    return (rows == ids[k : k + 1]).astype(jnp.float32).astype(jnp.bfloat16)


def hidden_kernel(first_k, per_k, top, experts, bits, me_ref, got_ref, *refs):
    weights, (send_ref, keep_ref, own_x, pair_x) = refs[:4], refs[4:]
    tokens = got_ref.shape[0]
    blocks, half, depth = weights[0].shape
    width = depth // experts
    step = pl.program_id(0)
    me = me_ref[0]

    @pl.when(step == 0)
    def _():
        columns, ids, _ = lane_tables(got_ref, 2 * width, top)
        low, high = columns[:width], columns[width:]
        first = me % 2 == 0
        for x_ref, part in (
            (own_x, jnp.where(first, low, high)),
            (pair_x, jnp.where(first, high, low)),
        ):
            wide = spread(part, experts)
            for k in range(per_k):
                x_ref[:, :, k * tokens : (k + 1) * tokens] = wide * named(
                    ids, first_k + k, experts
                )

    lanes = own_x.shape[2]
    result = jnp.zeros((2 * blocks * half, lanes), jnp.float32)
    for at, x_ref in ((0, own_x), (2, pair_x)):
        both = [w_ref[...].reshape(blocks * half, depth) for w_ref in weights[at : at + 2]]
        result = result + jnp.dot(
            jnp.concatenate(both, axis=0),
            x_ref[...].reshape(depth, lanes),
            preferred_element_type=jnp.float32,
        )
    count = send_ref.shape[0]
    for b in range(blocks):
        gate = result[b * half : (b + 1) * half]
        up = result[(blocks + b) * half : (blocks + b + 1) * half]
        place = flipped((step * blocks + b) ^ (me // 2), bits)

        @pl.when(place < count)
        def _():
            keep_ref[place, :half] = gate
            keep_ref[place, half:] = up

        @pl.when(place >= count)
        def _():
            send_ref[place - count, :half] = gate.astype(jnp.bfloat16)
            send_ref[place - count, half:] = up.astype(jnp.bfloat16)


def left_terms(chunks, first_k, parts, top, experts, width, got_ref, pieces, left):
    tokens = got_ref.shape[0]
    half = pieces[0].shape[-2] // 2
    _, ids, w = lane_tables(got_ref, width, top)
    at = first_k
    for c, per_k in enumerate(chunks):
        hidden = pieces[c * parts][0].astype(jnp.float32)
        for piece in pieces[c * parts + 1 : (c + 1) * parts]:
            hidden = hidden + piece[0].astype(jnp.float32)
        gate, up = hidden[:half], hidden[half:]
        activated = gate / (1.0 + jnp.exp(-gate)) * up
        for k in range(per_k):
            mine = activated[:, k * tokens : (k + 1) * tokens] * w[at : at + 1]
            term = spread(mine, experts) * named(ids, at, experts)
            left = term if left is None else left + term
            at += 1
    return left


def left_kernel(chunks, parts, top, experts, got_ref, *refs):
    width = got_ref.shape[1] - LANES
    refs[-1][...] = left_terms(chunks, 0, parts, top, experts, width, got_ref, refs[:-1], None)


def down_kernel(chunk, first_k, parts, top, experts, base, bits, *refs):
    me_ref, slot_ref, got_ref, before_ref, down_ref, scale_ref = refs[:6]
    pieces = refs[6:-5]
    send_ref, keep_ref, left_ref, part_ref, expert_ref = refs[-5:]
    tokens = got_ref.shape[0]
    width = got_ref.shape[1] - LANES

    @pl.when(pl.program_id(0) == 0)
    def _():
        for e in range(experts):
            expert_ref[slot_ref[e]] = e
        left = left_terms(
            (chunk,), first_k, parts, top, experts, width, got_ref, pieces, before_ref[...]
        )
        left_ref[...] = left.reshape(-1, tokens).T

    part_ref[...] = jnp.dot(left_ref[...], down_ref[...], preferred_element_type=jnp.float32)
    me = me_ref[0]
    count = send_ref.shape[0]
    rows = tokens // (2 * count)
    for place in range(2 * count):
        out_ref = keep_ref if place < count else send_ref
        d = flipped(place, bits) ^ me
        at = pl.multiple_of(d * rows, rows)
        for b in range(base // rows):
            out_ref[place % count, b * rows : (b + 1) * rows, :] = part_ref[
                pl.ds(at, rows), b * LANES : (b + 1) * LANES
            ]
        out_ref[place % count, base:, :] = scale_ref[expert_ref[d], 0].astype(jnp.float32)


def finish_kernel(gate_cols, gate_factor, down_factor, base, extra, *refs):
    pieces, (out_ref, scale_ref) = refs[:-2], refs[-2:]
    rows, _ = out_ref.shape
    steps = pieces[0].shape[1] // (base + extra)
    for s in range(steps):
        low = s * (base + extra)
        middle, high = low + base, low + base + extra
        total = pieces[0][0, low:middle].astype(jnp.float32)
        largest = pieces[0][0, middle:high].astype(jnp.float32)
        for piece in pieces[1:]:
            total = total + piece[0, low:middle].astype(jnp.float32)
            largest = jnp.maximum(largest, piece[0, middle:high].astype(jnp.float32))
        for q in range(base // rows):
            at = (s * (base // rows) + q) * LANES
            out_ref[:, at : at + LANES] = total[q * rows : (q + 1) * rows].astype(jnp.bfloat16)
        for q in range(extra):
            at = (s * extra + q) * LANES
            if at < scale_ref.shape[1]:
                factor = gate_factor if at < gate_cols else down_factor
                scale_ref[:, at : at + LANES] = largest[q : q + 1] * factor


def scatter(send, keep, n, first_bit, stages, merge):
    whole, pieces, shift = [keep], [keep], first_bit
    for stage, bits in enumerate(stages):
        count = 2**bits
        if stage:
            size = pieces[0].shape[0] // count
            send = [merge([p[m * size : (m + 1) * size] for p in pieces]) for m in range(1, count)]
            pieces = [p[:size] for p in pieces]
        for m in range(1, count):
            mask = flipped(m, bits) << shift
            got = lax.ppermute(send[m - 1], "ep", [(i, i ^ mask) for i in range(n)])
            whole.append(got)
            pieces.append(got)
        shift += bits
    return whole


def first_slot(piece):
    return pl.BlockSpec((1,) + piece.shape[1:], lambda *_: (0,) * piece.ndim)


def add_up(terms):
    return sum(t.astype(jnp.float32) for t in terms).astype(jnp.bfloat16)


def column_max(w, parts):
    rows, experts, cols = w.shape
    tile = cols // parts
    return pl.pallas_call(
        max_kernel,
        grid=(parts,),
        out_shape=jax.ShapeDtypeStruct((experts, cols), jnp.bfloat16),
        in_specs=[pl.BlockSpec((rows, experts, tile), lambda i: (0, 0, i))],
        out_specs=pl.BlockSpec((experts, tile), lambda i: (0, i)),
        compiler_params=params(12),
        cost_estimate=pl.CostEstimate(
            flops=2 * w.size, bytes_accessed=2 * w.size, transcendentals=0
        ),
    )(w)


def row_shards(tokens, gate_up, down_proj, expert_ids, gate_weights, owner_slot):
    return row_path(tokens, gate_up, down_proj, expert_ids, gate_weights, owner_slot)


def row_path(tokens, gate_up, down_proj, expert_ids, gate_weights, owner_slot):
    n = lax.axis_size("ep")
    bits = n.bit_length() - 1
    tok_rows, model_width = tokens.shape
    top = expert_ids.shape[1]
    gate_rows, experts, gate_cols = gate_up.shape
    down_rows, _, _ = down_proj.shape
    all_tokens = n * tok_rows
    depth = gate_rows * experts
    chunks = CHUNKS if top == sum(CHUNKS) else (top,)
    me = lax.axis_index("ep").astype(jnp.int32).reshape(1)

    packed = pl.pallas_call(
        pack_kernel,
        out_shape=jax.ShapeDtypeStruct((n, tok_rows, 2 * gate_rows + LANES), jnp.bfloat16),
        in_specs=[vmem()] * 3,
        out_specs=vmem(),
        compiler_params=params(62),
    )(tokens, expert_ids.T, gate_weights.T)
    got = lax.all_to_all(packed, "ep", split_axis=0, concat_axis=0, tiled=True)
    got = got.reshape(all_tokens, 2 * gate_rows + LANES)

    group = 8 if n % 8 == 0 else 4
    per_half = n // group
    block = pl.BlockSpec((group // 2, down_rows, depth), lambda i: (i, 0, 0))
    half_shape = jax.ShapeDtypeStruct((n // 2, down_rows, depth), jnp.bfloat16)
    own, pair = [], []
    for half in range(2):
        send, keep = pl.pallas_call(
            prep_kernel,
            grid=(per_half,),
            out_shape=(half_shape,) * 2,
            in_specs=[
                smem(),
                pl.BlockSpec(
                    (gate_rows, experts, group * down_rows),
                    lambda i, half=half: (0, 0, half * per_half + i),
                ),
            ],
            out_specs=(block,) * 2,
            compiler_params=params(PREP_MIB),
            cost_estimate=pl.CostEstimate(
                flops=gate_up.size, bytes_accessed=2 * gate_up.size, transcendentals=0
            ),
        )(me, gate_up)
        pair.append(lax.ppermute(send, "ep", [(i, i ^ 1) for i in range(n)]))
        own.append(keep)

    blocks = BLOCKS if (n // 2) % BLOCKS == 0 else 2
    all_pieces, first_k = [], 0
    for per_k in chunks:
        lanes = per_k * all_tokens
        shape = (n // 4, 2 * down_rows, lanes)
        send, keep = pl.pallas_call(
            functools.partial(hidden_kernel, first_k, per_k, top, experts, bits - 1),
            grid=(n // 2 // blocks,),
            out_shape=(
                jax.ShapeDtypeStruct(shape, jnp.bfloat16),
                jax.ShapeDtypeStruct(shape, jnp.float32),
            ),
            in_specs=[smem(), vmem()]
            + [pl.BlockSpec((blocks, down_rows, depth), lambda i: (i, 0, 0))] * 4,
            out_specs=(pl.BlockSpec(shape, lambda i: (0, 0, 0)),) * 2,
            scratch_shapes=[pltpu.VMEM((gate_rows, experts, lanes), jnp.bfloat16)] * 2,
            compiler_params=params(34),
            cost_estimate=pl.CostEstimate(
                flops=2 * depth * gate_cols * lanes,
                bytes_accessed=2 * depth * gate_cols + 3 * gate_cols * lanes // 2,
                transcendentals=0,
            ),
        )(me, got, *own, *pair)
        first_k += per_k
        all_pieces += scatter([send], keep, n, 1, HIDDEN_STAGES(bits - 1), add_up)

    parts = len(all_pieces) // len(chunks)
    scale_cols = gate_cols + model_width
    steps = OUT_STEPS if model_width % (OUT_STEPS * LANES) == 0 else 1
    base = tok_rows * model_width // LANES // steps
    extra = -(-scale_cols // (8 * steps * LANES)) * 8
    gate_max = column_max(gate_up, 2)
    down_max = column_max(down_proj, 2)
    local_max = jnp.concatenate(
        [
            gate_max,
            down_max,
            jnp.zeros((experts, steps * extra * LANES - scale_cols), jnp.bfloat16),
        ],
        axis=1,
    ).reshape(experts, steps, extra, LANES)

    early, late = all_pieces[:-parts], all_pieces[-parts:]
    before = pl.pallas_call(
        functools.partial(left_kernel, chunks[:-1], parts, top, experts),
        grid=(1,),
        out_shape=jax.ShapeDtypeStruct((down_rows, experts, all_tokens), jnp.bfloat16),
        in_specs=[vmem()] + [first_slot(p) for p in early],
        out_specs=vmem(),
        compiler_params=params(16),
    )(got, *early)
    shape = (n // 2, steps * (base + extra), LANES)
    out_block = pl.BlockSpec((n // 2, base + extra, LANES), lambda i: (0, i, 0))
    send, keep = pl.pallas_call(
        functools.partial(
            down_kernel, chunks[-1], top - chunks[-1], parts, top, experts, base, bits
        ),
        grid=(steps,),
        out_shape=(jax.ShapeDtypeStruct(shape, jnp.float32),) * 2,
        in_specs=[
            smem(),
            smem(),
            vmem(),
            vmem(),
            pl.BlockSpec((down_rows * experts, model_width // steps), lambda i: (0, i)),
            pl.BlockSpec((experts, 1, extra, LANES), lambda i: (0, i, 0, 0)),
        ]
        + [first_slot(p) for p in late],
        out_specs=(out_block,) * 2,
        scratch_shapes=[
            pltpu.VMEM((all_tokens, down_rows * experts), jnp.bfloat16),
            pltpu.VMEM((all_tokens, model_width // steps), jnp.float32),
            pltpu.SMEM((n,), jnp.int32),
        ],
        compiler_params=params(20),
    )(
        me,
        owner_slot,
        got,
        before,
        down_proj.reshape(down_rows * experts, model_width),
        local_max,
        *late,
    )

    def merge(terms):
        row = lax.broadcasted_iota(jnp.int32, terms[0].shape, 1) % (base + extra)
        terms = [t.astype(jnp.float32) for t in terms]
        return jnp.where(row < base, sum(terms), functools.reduce(jnp.maximum, terms)).astype(
            jnp.bfloat16
        )

    pieces = scatter([send], keep, n, 0, OUTPUT_STAGES(bits), merge)
    return pl.pallas_call(
        functools.partial(
            finish_kernel,
            gate_cols,
            math.sqrt(gate_rows * n),
            math.sqrt(down_rows * n),
            base,
            extra,
        ),
        grid=(1,),
        out_shape=(
            jax.ShapeDtypeStruct((tok_rows, model_width), jnp.bfloat16),
            jax.ShapeDtypeStruct((1, scale_cols), jnp.float32),
        ),
        in_specs=[first_slot(p) for p in pieces],
        out_specs=(vmem(),) * 2,
        compiler_params=params(8),
    )(*pieces)


def HIDDEN_STAGES(bits):
    return [1] * bits


def OUTPUT_STAGES(bits):
    return [1] * bits


def shards(tokens, gate_up, down_proj, expert_ids, gate_weights, owner_slot):
    n = lax.axis_size("ep")
    tok_rows, model_width = tokens.shape
    top = expert_ids.shape[1]
    gate_rows, experts, gate_cols = gate_up.shape
    down_rows = down_proj.shape[0]
    fits = (
        n >= 2
        and n & (n - 1) == 0
        and experts == n
        and experts % 16 == 0
        and tok_rows % 16 == 0
        and gate_rows % LANES == 0
        and down_rows % 16 == 0
        and n % 4 == 0
        and model_width % LANES == 0
        and gate_cols % LANES == 0
        and 3 * top <= LANES
        and experts <= 256
    )
    path = row_shards if fits else owner_shards
    return path(tokens, gate_up, down_proj, expert_ids, gate_weights, owner_slot)


def solution(mesh):
    in_specs = (
        P(("parts", "ep"), None),
        P(("parts", "ep"), None, None),
        P(("parts", "ep"), None, None),
        P(("parts", "ep"), None),
        P(("parts", "ep"), None),
        P("parts"),
    )
    out_specs = (P(("parts", "ep"), None), P(("parts", "ep"), None))
    return jax.shard_map(
        shards, mesh=mesh, in_specs=in_specs, out_specs=out_specs, check_vma=False
    )
```

```python
import functools
import math

import jax
import jax.numpy as jnp
from jax import lax
from jax.experimental import pallas as pl
from jax.experimental.pallas import tpu as pltpu
from jax.sharding import PartitionSpec as P


LANES = 128
CHUNKS = ((2, 0), (3, 0), (1, 1), (2, 0))
BLOCKS = 4
OUT_STEPS = 4
PREP_MIB = 58


def expert_block(arrived, held_up, held_down):
    hidden = jnp.einsum("rjd,djf->rjf", arrived, held_up, preferred_element_type=jnp.float32)
    ffn_width = held_up.shape[2] // 2
    activated = (jax.nn.silu(hidden[..., :ffn_width]) * hidden[..., ffn_width:]).astype(
        jnp.bfloat16
    )
    return jnp.einsum(
        "rjf,fjd->rjd", activated, held_down, preferred_element_type=jnp.float32
    ).astype(jnp.bfloat16)


def column_scales(gate_up, down_proj):
    gate_scale = jnp.max(jnp.abs(gate_up), axis=0).astype(jnp.float32) * math.sqrt(gate_up.shape[0])
    down_scale = jnp.max(jnp.abs(down_proj), axis=0).astype(jnp.float32) * math.sqrt(
        down_proj.shape[0]
    )
    return jnp.concatenate([gate_scale, down_scale], axis=1)


def owner_shards(tokens, gate_up, down_proj, expert_ids, gate_weights, owner_slot):
    tok_rows, model_width = tokens.shape
    top_count = expert_ids.shape[1]
    slots_all = gate_up.shape[1]
    devices = lax.axis_size("ep")
    own_count = slots_all // devices
    capacity = 2 * tok_rows * top_count // slots_all
    experts_iota = jnp.arange(slots_all, dtype=jnp.int32)
    inverse = jnp.zeros((slots_all,), jnp.int32).at[owner_slot].set(experts_iota)
    flat_ids = expert_ids.reshape(-1)
    one_hot = (flat_ids[:, None] == experts_iota[None, :]).astype(jnp.int32)
    slot_rank = jnp.sum((jnp.cumsum(one_hot, axis=0) - 1) * one_hot, axis=1)
    position = slot_rank * slots_all + flat_ids
    source_rows = jnp.repeat(tokens, top_count, axis=0)
    outbox = (
        jnp.zeros((capacity * slots_all, model_width), jnp.bfloat16).at[position].set(source_rows)
    )
    outbox = outbox.reshape(capacity, slots_all, model_width)
    held_up, held_down = (
        lax.all_to_all(gate_up, "ep", split_axis=1, concat_axis=0, tiled=True),
        lax.all_to_all(down_proj, "ep", split_axis=1, concat_axis=0, tiled=True),
    )
    arrived = lax.all_to_all(outbox, "ep", split_axis=1, concat_axis=0, tiled=True)
    expert_out = expert_block(arrived, held_up, held_down)
    returned = lax.all_to_all(expert_out, "ep", split_axis=0, concat_axis=1, tiled=True).reshape(
        capacity * slots_all, model_width
    )
    picked = returned[position].astype(jnp.float32).reshape(tok_rows, top_count, model_width)
    moe_out = jnp.sum(picked * gate_weights[:, :, None], axis=1).astype(jnp.bfloat16)
    scales = column_scales(held_up, held_down)
    every_row = lax.all_gather(scales, "ep", axis=0, tiled=True)
    mine = lax.dynamic_slice_in_dim(inverse, lax.axis_index("ep") * own_count, own_count)
    scales = jnp.take(every_row, mine, axis=0)
    return (moe_out, scales)


def params(mib):
    return pltpu.CompilerParams(vmem_limit_bytes=mib * 1024 * 1024)


def bit_order(bits, turn):
    return tuple((b + turn) % bits for b in range(bits))


def place_of(slot, order):
    top = len(order) - 1
    return sum(((slot >> bit) & 1) << (top - i) for i, bit in enumerate(order))


def slot_at(place, order):
    top = len(order) - 1
    return sum(((place >> (top - i)) & 1) << bit for i, bit in enumerate(order))


def vmem():
    return pl.BlockSpec(memory_space=pltpu.VMEM)


def smem():
    return pl.BlockSpec(memory_space=pltpu.SMEM)


def pack_kernel(tok_ref, ids_ref, w_ref, out_ref):
    n = out_ref.shape[0]
    width = out_ref.shape[2] - LANES
    top, rows = ids_ref.shape
    w = w_ref[...]
    w_hi = w.astype(jnp.bfloat16).astype(jnp.float32)
    meta = jnp.concatenate(
        [
            ids_ref[...].astype(jnp.float32),
            w_hi,
            w - w_hi,
            jnp.zeros((LANES - 3 * top, rows), jnp.float32),
        ],
        axis=0,
    ).T.astype(jnp.bfloat16)
    for d in range(n):
        pair = d // 2
        out_ref[d, :, :width] = tok_ref[:, pair * width : (pair + 1) * width]
        out_ref[d, :, width:] = meta


def prep_kernel(me_ref, gate_ref, send_ref, keep_ref):
    rows, experts, cols = gate_ref.shape
    turned = gate_ref[...].reshape(rows * experts, cols).T
    half = keep_ref.shape[1]
    parity = me_ref[0] % 2
    for d in range(cols // half):
        part = turned[d * half : (d + 1) * half]

        @pl.when(parity == d % 2)
        def _():
            keep_ref[d // 2] = part

        @pl.when(parity != d % 2)
        def _():
            send_ref[d // 2] = part


def max_kernel(w_ref, max_ref):
    top = jnp.abs(w_ref[0])
    for r in range(1, w_ref.shape[0]):
        top = jnp.maximum(top, jnp.abs(w_ref[r]))
    max_ref[...] = top


def lane_tables(got_ref, width, top):
    turned = got_ref[...].astype(jnp.float32).T
    ids = turned[width : width + top]
    w = turned[width + top : width + 2 * top] + turned[width + 2 * top : width + 3 * top]
    return turned[:width], ids, w


def spread(values, experts):
    rows, lanes = values.shape
    pick = lax.broadcasted_iota(jnp.int32, (rows * experts, rows), 0) // experts
    hot = (pick == lax.broadcasted_iota(jnp.int32, (rows * experts, rows), 1)).astype(
        jnp.float32
    ).astype(jnp.bfloat16)
    wide = jnp.dot(hot, values.astype(jnp.bfloat16), preferred_element_type=jnp.float32)
    return wide.astype(jnp.bfloat16).reshape(rows, experts, lanes)


def named(ids, k, experts):
    rows = lax.broadcasted_iota(jnp.int32, (experts, ids.shape[1]), 0).astype(jnp.float32)
    return (rows == ids[k : k + 1]).astype(jnp.float32).astype(jnp.bfloat16)


def hidden_kernel(
    first_k, per_k, top, experts, order, sides, has_base, me_ref, got_ref, *refs
):
    weights, refs = refs[: 2 * len(sides)], refs[2 * len(sides) :]
    base_ref, refs = (refs[0], refs[1:]) if has_base else (None, refs)
    x_refs, outs = refs[-len(sides) :], refs[: -len(sides)]
    tokens = got_ref.shape[0]
    blocks, half, depth = weights[0].shape
    width = depth // experts
    step = pl.program_id(0)
    me = me_ref[0]

    @pl.when(step == 0)
    def _():
        columns, ids, _ = lane_tables(got_ref, 2 * width, top)
        low, high = columns[:width], columns[width:]
        for side, x_ref in zip(sides, x_refs):
            wide = spread(jnp.where(me % 2 == side, low, high), experts)
            for k in range(per_k):
                x_ref[:, :, k * tokens : (k + 1) * tokens] = wide * named(
                    ids, first_k + k, experts
                )

    lanes = x_refs[0].shape[2]
    rows = blocks * half
    result = base_ref[...].reshape(2 * rows, lanes) if has_base else None
    for at, x_ref in enumerate(x_refs):
        both = [w_ref[...].reshape(rows, depth) for w_ref in weights[2 * at : 2 * at + 2]]
        term = jnp.dot(
            jnp.concatenate(both, axis=0),
            x_ref[...].reshape(depth, lanes),
            preferred_element_type=jnp.float32,
        )
        result = term if result is None else result + term
    if len(outs) == 1:
        outs[0][...] = result.reshape(outs[0].shape)
        return
    send_ref, keep_ref = outs
    count = send_ref.shape[0]
    for b in range(blocks):
        gate = result[b * half : (b + 1) * half]
        up = result[rows + b * half : rows + (b + 1) * half]
        place = place_of((step * blocks + b) ^ (me // 2), order)

        @pl.when(place < count)
        def _():
            keep_ref[place, :half] = gate
            keep_ref[place, half:] = up

        @pl.when(place >= count)
        def _():
            send_ref[place - count, :half] = gate.astype(jnp.bfloat16)
            send_ref[place - count, half:] = up.astype(jnp.bfloat16)


def left_terms(chunks, first_k, parts, top, experts, width, got_ref, pieces, left):
    tokens = got_ref.shape[0]
    half = pieces[0].shape[-2] // 2
    _, ids, w = lane_tables(got_ref, width, top)
    at = first_k
    for c, per_k in enumerate(chunks):
        hidden = pieces[c * parts][0].astype(jnp.float32)
        for piece in pieces[c * parts + 1 : (c + 1) * parts]:
            hidden = hidden + piece[0].astype(jnp.float32)
        gate, up = hidden[:half], hidden[half:]
        activated = gate / (1.0 + jnp.exp(-gate)) * up
        for k in range(per_k):
            mine = activated[:, k * tokens : (k + 1) * tokens] * w[at : at + 1]
            term = spread(mine, experts) * named(ids, at, experts)
            left = term if left is None else left + term
            at += 1
    return left


def left_kernel(chunks, parts, top, experts, got_ref, *refs):
    width = got_ref.shape[1] - LANES
    refs[-1][...] = left_terms(chunks, 0, parts, top, experts, width, got_ref, refs[:-1], None)


def down_kernel(chunk, first_k, parts, top, experts, base, orders, *refs):
    me_ref, slot_ref, got_ref, before_ref, down_ref, scale_ref = refs[:6]
    pieces = refs[6:-5]
    send_ref, keep_ref, left_ref, part_ref, expert_ref = refs[-5:]
    tokens = got_ref.shape[0]
    width = got_ref.shape[1] - LANES

    @pl.when(pl.program_id(0) == 0)
    def _():
        for e in range(experts):
            expert_ref[slot_ref[e]] = e
        left = left_terms(
            (chunk,), first_k, parts, top, experts, width, got_ref, pieces, before_ref[...]
        )
        left_ref[...] = left.reshape(-1, tokens).T

    part_ref[...] = jnp.dot(left_ref[...], down_ref[...], preferred_element_type=jnp.float32)
    me = me_ref[0]
    count = send_ref.shape[0]
    rows = tokens // (2 * count)
    for place in range(2 * count):
        out_ref = keep_ref if place < count else send_ref
        early, late = (slot_at(place, order) for order in orders)
        d = jnp.where(pl.program_id(0) < pl.num_programs(0) // 2, early, late) ^ me
        at = pl.multiple_of(d * rows, rows)
        for b in range(base // rows):
            out_ref[place % count, b * rows : (b + 1) * rows, :] = part_ref[
                pl.ds(at, rows), b * LANES : (b + 1) * LANES
            ]
        out_ref[place % count, base:, :] = scale_ref[expert_ref[d], 0].astype(jnp.float32)


def finish_kernel(gate_cols, gate_factor, down_factor, base, extra, count, *refs):
    pieces, (out_ref, scale_ref) = refs[:-2], refs[-2:]
    rows, _ = out_ref.shape
    steps = pieces[0].shape[1] // (base + extra)
    shared, rest = pieces[:2], pieces[2:]
    for s in range(steps):
        low = s * (base + extra)
        terms = [piece[0, low : low + base + extra].astype(jnp.float32) for piece in shared]
        low = s % (steps // 2) * (base + extra)
        part = rest[:count] if s < steps // 2 else rest[count:]
        terms += [piece[0, low : low + base + extra].astype(jnp.float32) for piece in part]
        total = sum(t[:base] for t in terms)
        largest = functools.reduce(jnp.maximum, [t[base:] for t in terms])
        for q in range(base // rows):
            at = (s * (base // rows) + q) * LANES
            out_ref[:, at : at + LANES] = total[q * rows : (q + 1) * rows].astype(jnp.bfloat16)
        for q in range(extra):
            at = (s * extra + q) * LANES
            if at < scale_ref.shape[1]:
                factor = gate_factor if at < gate_cols else down_factor
                scale_ref[:, at : at + LANES] = largest[q : q + 1] * factor


def scatter(send, pieces, n, first_bit, order, merge):
    whole = []
    for bit in order:
        if send is None:
            size = pieces[0].shape[0] // 2
            send = merge([p[size:] for p in pieces])
            pieces = [p[:size] for p in pieces]
        mask = 1 << (bit + first_bit)
        got = lax.ppermute(send, "ep", [(i, i ^ mask) for i in range(n)])
        whole.append(got)
        pieces = pieces + [got]
        send = None
    return whole


def first_slot(piece):
    return pl.BlockSpec((1,) + piece.shape[1:], lambda *_: (0,) * piece.ndim)


def add_up(terms):
    return sum(t.astype(jnp.float32) for t in terms).astype(jnp.bfloat16)


def column_max(w, parts):
    rows, experts, cols = w.shape
    tile = cols // parts
    return pl.pallas_call(
        max_kernel,
        grid=(parts,),
        out_shape=jax.ShapeDtypeStruct((experts, cols), jnp.bfloat16),
        in_specs=[pl.BlockSpec((rows, experts, tile), lambda i: (0, 0, i))],
        out_specs=pl.BlockSpec((experts, tile), lambda i: (0, i)),
        compiler_params=params(12),
        cost_estimate=pl.CostEstimate(
            flops=2 * w.size, bytes_accessed=2 * w.size, transcendentals=0
        ),
    )(w)


def row_shards(tokens, gate_up, down_proj, expert_ids, gate_weights, owner_slot):
    return row_path(tokens, gate_up, down_proj, expert_ids, gate_weights, owner_slot)


def row_path(tokens, gate_up, down_proj, expert_ids, gate_weights, owner_slot):
    n = lax.axis_size("ep")
    bits = n.bit_length() - 1
    tok_rows, model_width = tokens.shape
    top = expert_ids.shape[1]
    gate_rows, experts, gate_cols = gate_up.shape
    down_rows, _, _ = down_proj.shape
    all_tokens = n * tok_rows
    depth = gate_rows * experts
    plan = CHUNKS if top == sum(size for size, _ in CHUNKS) else ((top, 0),)
    chunks = tuple(size for size, _ in plan)
    me = lax.axis_index("ep").astype(jnp.int32).reshape(1)

    packed = pl.pallas_call(
        pack_kernel,
        out_shape=jax.ShapeDtypeStruct((n, tok_rows, 2 * gate_rows + LANES), jnp.bfloat16),
        in_specs=[vmem()] * 3,
        out_specs=vmem(),
        compiler_params=params(62),
    )(tokens, expert_ids.T, gate_weights.T)
    got = lax.all_to_all(packed, "ep", split_axis=0, concat_axis=0, tiled=True)
    got = got.reshape(all_tokens, 2 * gate_rows + LANES)

    group = 8 if n % 8 == 0 else 4
    per_half = n // group
    block = pl.BlockSpec((group // 2, down_rows, depth), lambda i: (i, 0, 0))
    half_shape = jax.ShapeDtypeStruct((n // 2, down_rows, depth), jnp.bfloat16)
    own, pair = [], []
    for half in range(2):
        send, keep = pl.pallas_call(
            prep_kernel,
            grid=(per_half,),
            out_shape=(half_shape,) * 2,
            in_specs=[
                smem(),
                pl.BlockSpec(
                    (gate_rows, experts, group * down_rows),
                    lambda i, half=half: (0, 0, half * per_half + i),
                ),
            ],
            out_specs=(block,) * 2,
            compiler_params=params(PREP_MIB),
            cost_estimate=pl.CostEstimate(
                flops=gate_up.size, bytes_accessed=2 * gate_up.size, transcendentals=0
            ),
        )(me, gate_up)
        pair.append(lax.ppermute(send, "ep", [(i, i ^ 1) for i in range(n)]))
        own.append(keep)

    blocks = BLOCKS if (n // 2) % BLOCKS == 0 else 2
    all_pieces, first_k = [], 0
    for c, (per_k, turn) in enumerate(plan):
        order = bit_order(bits - 1, turn)
        lanes = per_k * all_tokens
        steps = n // 2 // blocks
        shape = (n // 4, 2 * down_rows, lanes)
        pieces_out = (
            jax.ShapeDtypeStruct(shape, jnp.bfloat16),
            jax.ShapeDtypeStruct(shape, jnp.float32),
        )
        pieces_spec = (pl.BlockSpec(shape, lambda i: (0, 0, 0)),) * 2
        part = (steps, 2 * blocks * down_rows, lanes)
        part_spec = pl.BlockSpec((1,) + part[1:], lambda i: (i, 0, 0))

        def hidden(sides, weights, base, out_shape, out_specs):
            return pl.pallas_call(
                functools.partial(
                    hidden_kernel,
                    first_k,
                    per_k,
                    top,
                    experts,
                    order,
                    sides,
                    len(base) == 1,
                ),
                grid=(steps,),
                out_shape=out_shape,
                in_specs=[smem(), vmem()]
                + [pl.BlockSpec((blocks, down_rows, depth), lambda i: (i, 0, 0))]
                * len(weights)
                + [part_spec] * len(base),
                out_specs=out_specs,
                scratch_shapes=[pltpu.VMEM((gate_rows, experts, lanes), jnp.bfloat16)]
                * len(sides),
                compiler_params=params(34),
                cost_estimate=pl.CostEstimate(
                    flops=depth * gate_cols * lanes * len(sides),
                    bytes_accessed=depth * gate_cols * len(sides)
                    + 3 * gate_cols * lanes // 2,
                    transcendentals=0,
                ),
            )(me, got, *weights, *base)

        if c:
            send, keep = hidden((0, 1), own + pair, [], pieces_out, pieces_spec)
        else:
            base = hidden((0,), own, [], jax.ShapeDtypeStruct(part, jnp.float32), part_spec)
            send, keep = hidden((1,), pair, [base], pieces_out, pieces_spec)
        first_k += per_k
        all_pieces += [keep] + scatter(send, [keep], n, 1, order, add_up)

    parts = len(all_pieces) // len(chunks)
    scale_cols = gate_cols + model_width
    steps = OUT_STEPS if model_width % (OUT_STEPS * LANES) == 0 else 2
    base = tok_rows * model_width // LANES // steps
    extra = -(-scale_cols // (8 * steps * LANES)) * 8
    gate_max = column_max(gate_up, 2)
    down_max = column_max(down_proj, 2)
    local_max = jnp.concatenate(
        [
            gate_max,
            down_max,
            jnp.zeros((experts, steps * extra * LANES - scale_cols), jnp.bfloat16),
        ],
        axis=1,
    ).reshape(experts, steps, extra, LANES)

    early, late = all_pieces[:-parts], all_pieces[-parts:]
    before = pl.pallas_call(
        functools.partial(left_kernel, chunks[:-1], parts, top, experts),
        grid=(1,),
        out_shape=jax.ShapeDtypeStruct((down_rows, experts, all_tokens), jnp.bfloat16),
        in_specs=[vmem()] + [first_slot(p) for p in early],
        out_specs=vmem(),
        compiler_params=params(16),
    )(got, *early)
    orders = [(0,) + tuple(b + 1 for b in bit_order(bits - 1, turn)) for turn in range(2)]
    shape = (n // 2, steps * (base + extra), LANES)
    out_block = pl.BlockSpec((n // 2, base + extra, LANES), lambda i: (0, i, 0))
    send, keep = pl.pallas_call(
        functools.partial(
            down_kernel, chunks[-1], top - chunks[-1], parts, top, experts, base, orders
        ),
        grid=(steps,),
        out_shape=(jax.ShapeDtypeStruct(shape, jnp.float32),) * 2,
        in_specs=[
            smem(),
            smem(),
            vmem(),
            vmem(),
            pl.BlockSpec((down_rows * experts, model_width // steps), lambda i: (0, i)),
            pl.BlockSpec((experts, 1, extra, LANES), lambda i: (0, i, 0, 0)),
        ]
        + [first_slot(p) for p in late],
        out_specs=(out_block,) * 2,
        scratch_shapes=[
            pltpu.VMEM((all_tokens, down_rows * experts), jnp.bfloat16),
            pltpu.VMEM((all_tokens, model_width // steps), jnp.float32),
            pltpu.SMEM((n,), jnp.int32),
        ],
        compiler_params=params(20),
    )(
        me,
        owner_slot,
        got,
        before,
        down_proj.reshape(down_rows * experts, model_width),
        local_max,
        *late,
    )

    def merge(terms):
        row = lax.broadcasted_iota(jnp.int32, terms[0].shape, 1) % (base + extra)
        terms = [t.astype(jnp.float32) for t in terms]
        return jnp.where(row < base, sum(terms), functools.reduce(jnp.maximum, terms)).astype(
            jnp.bfloat16
        )

    pieces = [keep] + scatter(send, [keep], n, 0, (0,), merge)
    middle = steps // 2 * (base + extra)
    for half, order in enumerate(orders):
        own = [p[:, half * middle : (half + 1) * middle] for p in pieces[:2]]
        pieces = pieces + scatter(None, own, n, 0, order[1:], merge)
    return pl.pallas_call(
        functools.partial(
            finish_kernel,
            gate_cols,
            math.sqrt(gate_rows * n),
            math.sqrt(down_rows * n),
            base,
            extra,
            bits - 1,
        ),
        grid=(1,),
        out_shape=(
            jax.ShapeDtypeStruct((tok_rows, model_width), jnp.bfloat16),
            jax.ShapeDtypeStruct((1, scale_cols), jnp.float32),
        ),
        in_specs=[first_slot(p) for p in pieces],
        out_specs=(vmem(),) * 2,
        compiler_params=params(10),
    )(*pieces)


def shards(tokens, gate_up, down_proj, expert_ids, gate_weights, owner_slot):
    n = lax.axis_size("ep")
    tok_rows, model_width = tokens.shape
    top = expert_ids.shape[1]
    gate_rows, experts, gate_cols = gate_up.shape
    down_rows = down_proj.shape[0]
    fits = (
        n >= 2
        and n & (n - 1) == 0
        and experts == n
        and experts % 16 == 0
        and tok_rows % 16 == 0
        and gate_rows % LANES == 0
        and down_rows % 16 == 0
        and n % 4 == 0
        and model_width % LANES == 0
        and gate_cols % LANES == 0
        and 3 * top <= LANES
        and experts <= 256
    )
    path = row_shards if fits else owner_shards
    return path(tokens, gate_up, down_proj, expert_ids, gate_weights, owner_slot)


def solution(mesh):
    in_specs = (
        P(("parts", "ep"), None),
        P(("parts", "ep"), None, None),
        P(("parts", "ep"), None, None),
        P(("parts", "ep"), None),
        P(("parts", "ep"), None),
        P("parts"),
    )
    out_specs = (P(("parts", "ep"), None), P(("parts", "ep"), None))
    return jax.shard_map(
        shards, mesh=mesh, in_specs=in_specs, out_specs=out_specs, check_vma=False
    )
```

```python
import functools
import math

import jax
import jax.numpy as jnp
from jax import lax
from jax.experimental import pallas as pl
from jax.experimental.pallas import tpu as pltpu
from jax.sharding import PartitionSpec as P


LANES = 128
CHUNKS = ((2, 0), (3, 0), (1, 1), (2, 0))
GROUPS = (1, 2, 1)
BLOCKS = 8
OUT_STEPS = 2
PREP_MIB = 58
HID_MIB = 34


def expert_block(arrived, held_up, held_down):
    hidden = jnp.einsum("rjd,djf->rjf", arrived, held_up, preferred_element_type=jnp.float32)
    ffn_width = held_up.shape[2] // 2
    activated = (jax.nn.silu(hidden[..., :ffn_width]) * hidden[..., ffn_width:]).astype(
        jnp.bfloat16
    )
    return jnp.einsum(
        "rjf,fjd->rjd", activated, held_down, preferred_element_type=jnp.float32
    ).astype(jnp.bfloat16)


def column_scales(gate_up, down_proj):
    gate_scale = jnp.max(jnp.abs(gate_up), axis=0).astype(jnp.float32) * math.sqrt(gate_up.shape[0])
    down_scale = jnp.max(jnp.abs(down_proj), axis=0).astype(jnp.float32) * math.sqrt(
        down_proj.shape[0]
    )
    return jnp.concatenate([gate_scale, down_scale], axis=1)


def owner_shards(tokens, gate_up, down_proj, expert_ids, gate_weights, owner_slot):
    tok_rows, model_width = tokens.shape
    top_count = expert_ids.shape[1]
    slots_all = gate_up.shape[1]
    devices = lax.axis_size("ep")
    own_count = slots_all // devices
    capacity = 2 * tok_rows * top_count // slots_all
    experts_iota = jnp.arange(slots_all, dtype=jnp.int32)
    inverse = jnp.zeros((slots_all,), jnp.int32).at[owner_slot].set(experts_iota)
    flat_ids = expert_ids.reshape(-1)
    one_hot = (flat_ids[:, None] == experts_iota[None, :]).astype(jnp.int32)
    slot_rank = jnp.sum((jnp.cumsum(one_hot, axis=0) - 1) * one_hot, axis=1)
    position = slot_rank * slots_all + flat_ids
    source_rows = jnp.repeat(tokens, top_count, axis=0)
    outbox = (
        jnp.zeros((capacity * slots_all, model_width), jnp.bfloat16).at[position].set(source_rows)
    )
    outbox = outbox.reshape(capacity, slots_all, model_width)
    held_up, held_down = (
        lax.all_to_all(gate_up, "ep", split_axis=1, concat_axis=0, tiled=True),
        lax.all_to_all(down_proj, "ep", split_axis=1, concat_axis=0, tiled=True),
    )
    arrived = lax.all_to_all(outbox, "ep", split_axis=1, concat_axis=0, tiled=True)
    expert_out = expert_block(arrived, held_up, held_down)
    returned = lax.all_to_all(expert_out, "ep", split_axis=0, concat_axis=1, tiled=True).reshape(
        capacity * slots_all, model_width
    )
    picked = returned[position].astype(jnp.float32).reshape(tok_rows, top_count, model_width)
    moe_out = jnp.sum(picked * gate_weights[:, :, None], axis=1).astype(jnp.bfloat16)
    scales = column_scales(held_up, held_down)
    every_row = lax.all_gather(scales, "ep", axis=0, tiled=True)
    mine = lax.dynamic_slice_in_dim(inverse, lax.axis_index("ep") * own_count, own_count)
    scales = jnp.take(every_row, mine, axis=0)
    return (moe_out, scales)


def params(mib):
    return pltpu.CompilerParams(vmem_limit_bytes=mib * 1024 * 1024)


def bit_order(bits, turn):
    return tuple((b + turn) % bits for b in range(bits))


def place_of(slot, order):
    top = len(order) - 1
    return sum(((slot >> bit) & 1) << (top - i) for i, bit in enumerate(order))


def slot_at(place, order):
    top = len(order) - 1
    return sum(((place >> (top - i)) & 1) << bit for i, bit in enumerate(order))


def vmem():
    return pl.BlockSpec(memory_space=pltpu.VMEM)


def smem():
    return pl.BlockSpec(memory_space=pltpu.SMEM)


def pack_kernel(tok_ref, ids_ref, w_ref, out_ref):
    n = out_ref.shape[0]
    width = out_ref.shape[2] - LANES
    top, rows = ids_ref.shape
    w = w_ref[...]
    w_hi = w.astype(jnp.bfloat16).astype(jnp.float32)
    meta = jnp.concatenate(
        [
            ids_ref[...].astype(jnp.float32),
            w_hi,
            w - w_hi,
            jnp.zeros((LANES - 3 * top, rows), jnp.float32),
        ],
        axis=0,
    ).T.astype(jnp.bfloat16)
    for d in range(n):
        pair = d // 2
        out_ref[d, :, :width] = tok_ref[:, pair * width : (pair + 1) * width]
        out_ref[d, :, width:] = meta


def prep_kernel(me_ref, gate_ref, send_ref, keep_ref):
    rows, experts, cols = gate_ref.shape
    turned = gate_ref[...].reshape(rows * experts, cols).T
    half = keep_ref.shape[1]
    parity = me_ref[0] % 2
    for d in range(cols // half):
        part = turned[d * half : (d + 1) * half]

        @pl.when(parity == d % 2)
        def _():
            keep_ref[d // 2] = part

        @pl.when(parity != d % 2)
        def _():
            send_ref[d // 2] = part


def max_kernel(w_ref, max_ref):
    top = jnp.abs(w_ref[0])
    for r in range(1, w_ref.shape[0]):
        top = jnp.maximum(top, jnp.abs(w_ref[r]))
    max_ref[...] = top


def lane_tables(got_ref, width, top):
    turned = got_ref[...].astype(jnp.float32).T
    ids = turned[width : width + top]
    w = turned[width + top : width + 2 * top] + turned[width + 2 * top : width + 3 * top]
    return turned[:width], ids, w


def spread(values, experts):
    rows, lanes = values.shape
    pick = lax.broadcasted_iota(jnp.int32, (rows * experts, rows), 0) // experts
    hot = (pick == lax.broadcasted_iota(jnp.int32, (rows * experts, rows), 1)).astype(
        jnp.float32
    ).astype(jnp.bfloat16)
    wide = jnp.dot(hot, values.astype(jnp.bfloat16), preferred_element_type=jnp.float32)
    return wide.astype(jnp.bfloat16).reshape(rows, experts, lanes)


def named(ids, k, experts):
    rows = lax.broadcasted_iota(jnp.int32, (experts, ids.shape[1]), 0).astype(jnp.float32)
    return (rows == ids[k : k + 1]).astype(jnp.float32).astype(jnp.bfloat16)


def hidden_kernel(
    first_k, parts, top, experts, sides, has_base, me_ref, got_ref, *refs
):
    weights, refs = refs[: 2 * len(sides)], refs[2 * len(sides) :]
    base_ref, refs = (refs[0], refs[1:]) if has_base else (None, refs)
    x_refs, outs = refs[-len(sides) :], refs[: -len(sides)]
    tokens = got_ref.shape[0]
    blocks, half, depth = weights[0].shape
    width = depth // experts
    step = pl.program_id(0)
    me = me_ref[0]

    @pl.when(step == 0)
    def _():
        columns, ids, _ = lane_tables(got_ref, 2 * width, top)
        low, high = columns[:width], columns[width:]
        for side, x_ref in zip(sides, x_refs):
            wide = spread(jnp.where(me % 2 == side, low, high), experts)
            for k in range(x_ref.shape[2] // tokens):
                x_ref[:, :, k * tokens : (k + 1) * tokens] = wide * named(
                    ids, first_k + k, experts
                )

    lanes = x_refs[0].shape[2]
    rows = blocks * half
    result = base_ref[...].reshape(2 * rows, lanes) if has_base else None
    for at, x_ref in enumerate(x_refs):
        both = [w_ref[...].reshape(rows, depth) for w_ref in weights[2 * at : 2 * at + 2]]
        term = jnp.dot(
            jnp.concatenate(both, axis=0),
            x_ref[...].reshape(depth, lanes),
            preferred_element_type=jnp.float32,
        )
        result = term if result is None else result + term
    if len(outs) == 1:
        outs[0][...] = result.reshape(outs[0].shape)
        return
    low = 0
    for at, (per_k, order) in enumerate(parts):
        send_ref, keep_ref = outs[2 * at : 2 * at + 2]
        piece = result[:, low * tokens : (low + per_k) * tokens]
        low += per_k
        count = send_ref.shape[0]
        for b in range(blocks):
            gate = piece[b * half : (b + 1) * half]
            up = piece[rows + b * half : rows + (b + 1) * half]
            place = place_of((step * blocks + b) ^ (me // 2), order)

            @pl.when(place < count)
            def _():
                keep_ref[place, :half] = gate
                keep_ref[place, half:] = up

            @pl.when(place >= count)
            def _():
                send_ref[place - count, :half] = gate.astype(jnp.bfloat16)
                send_ref[place - count, half:] = up.astype(jnp.bfloat16)


def left_terms(chunks, first_k, parts, top, experts, width, got_ref, pieces, left):
    tokens = got_ref.shape[0]
    half = pieces[0].shape[-2] // 2
    _, ids, w = lane_tables(got_ref, width, top)
    at = first_k
    for c, per_k in enumerate(chunks):
        hidden = pieces[c * parts][0].astype(jnp.float32)
        for piece in pieces[c * parts + 1 : (c + 1) * parts]:
            hidden = hidden + piece[0].astype(jnp.float32)
        gate, up = hidden[:half], hidden[half:]
        activated = gate / (1.0 + jnp.exp(-gate)) * up
        for k in range(per_k):
            mine = activated[:, k * tokens : (k + 1) * tokens] * w[at : at + 1]
            term = spread(mine, experts) * named(ids, at, experts)
            left = term if left is None else left + term
            at += 1
    return left


def left_kernel(chunks, parts, top, experts, got_ref, *refs):
    width = got_ref.shape[1] - LANES
    refs[-1][...] = left_terms(chunks, 0, parts, top, experts, width, got_ref, refs[:-1], None)


def down_kernel(chunk, first_k, parts, top, experts, base, orders, *refs):
    me_ref, slot_ref, got_ref, before_ref, down_ref, scale_ref = refs[:6]
    pieces = refs[6:-5]
    send_ref, keep_ref, left_ref, part_ref, expert_ref = refs[-5:]
    tokens = got_ref.shape[0]
    width = got_ref.shape[1] - LANES

    @pl.when(pl.program_id(0) == 0)
    def _():
        for e in range(experts):
            expert_ref[slot_ref[e]] = e
        left = left_terms(
            (chunk,), first_k, parts, top, experts, width, got_ref, pieces, before_ref[...]
        )
        left_ref[...] = left.reshape(-1, tokens).T

    part_ref[...] = jnp.dot(left_ref[...], down_ref[...], preferred_element_type=jnp.float32)
    me = me_ref[0]
    count = send_ref.shape[0]
    rows = tokens // (2 * count)
    for place in range(2 * count):
        out_ref = keep_ref if place < count else send_ref
        early, late = (slot_at(place, order) for order in orders)
        d = jnp.where(pl.program_id(0) < pl.num_programs(0) // 2, early, late) ^ me
        at = pl.multiple_of(d * rows, rows)
        for b in range(base // rows):
            out_ref[place % count, b * rows : (b + 1) * rows, :] = part_ref[
                pl.ds(at, rows), b * LANES : (b + 1) * LANES
            ]
        out_ref[place % count, base:, :] = scale_ref[expert_ref[d], 0].astype(jnp.float32)


def finish_kernel(gate_cols, gate_factor, down_factor, base, extra, count, *refs):
    pieces, (out_ref, scale_ref) = refs[:-2], refs[-2:]
    rows, _ = out_ref.shape
    steps = pieces[0].shape[1] // (base + extra)
    shared, rest = pieces[:2], pieces[2:]
    for s in range(steps):
        low = s * (base + extra)
        terms = [piece[0, low : low + base + extra].astype(jnp.float32) for piece in shared]
        low = s % (steps // 2) * (base + extra)
        part = rest[:count] if s < steps // 2 else rest[count:]
        terms += [piece[0, low : low + base + extra].astype(jnp.float32) for piece in part]
        total = sum(t[:base] for t in terms)
        largest = functools.reduce(jnp.maximum, [t[base:] for t in terms])
        for q in range(base // rows):
            at = (s * (base // rows) + q) * LANES
            out_ref[:, at : at + LANES] = total[q * rows : (q + 1) * rows].astype(jnp.bfloat16)
        for q in range(extra):
            at = (s * extra + q) * LANES
            if at < scale_ref.shape[1]:
                factor = gate_factor if at < gate_cols else down_factor
                scale_ref[:, at : at + LANES] = largest[q : q + 1] * factor


def scatter(send, pieces, n, first_bit, order, merge):
    whole = []
    for bit in order:
        if send is None:
            size = pieces[0].shape[0] // 2
            send = merge([p[size:] for p in pieces])
            pieces = [p[:size] for p in pieces]
        mask = 1 << (bit + first_bit)
        got = lax.ppermute(send, "ep", [(i, i ^ mask) for i in range(n)])
        whole.append(got)
        pieces = pieces + [got]
        send = None
    return whole


def first_slot(piece):
    return pl.BlockSpec((1,) + piece.shape[1:], lambda *_: (0,) * piece.ndim)


def add_up(terms):
    return sum(t.astype(jnp.float32) for t in terms).astype(jnp.bfloat16)


def column_max(w, parts):
    rows, experts, cols = w.shape
    tile = cols // parts
    return pl.pallas_call(
        max_kernel,
        grid=(parts,),
        out_shape=jax.ShapeDtypeStruct((experts, cols), jnp.bfloat16),
        in_specs=[pl.BlockSpec((rows, experts, tile), lambda i: (0, 0, i))],
        out_specs=pl.BlockSpec((experts, tile), lambda i: (0, i)),
        compiler_params=params(12),
        cost_estimate=pl.CostEstimate(
            flops=2 * w.size, bytes_accessed=2 * w.size, transcendentals=0
        ),
    )(w)


def row_shards(tokens, gate_up, down_proj, expert_ids, gate_weights, owner_slot):
    return row_path(tokens, gate_up, down_proj, expert_ids, gate_weights, owner_slot)


def row_path(tokens, gate_up, down_proj, expert_ids, gate_weights, owner_slot):
    n = lax.axis_size("ep")
    bits = n.bit_length() - 1
    tok_rows, model_width = tokens.shape
    top = expert_ids.shape[1]
    gate_rows, experts, gate_cols = gate_up.shape
    down_rows, _, _ = down_proj.shape
    all_tokens = n * tok_rows
    depth = gate_rows * experts
    plan = CHUNKS if top == sum(size for size, _ in CHUNKS) else ((top, 0),)
    chunks = tuple(size for size, _ in plan)
    me = lax.axis_index("ep").astype(jnp.int32).reshape(1)

    packed = pl.pallas_call(
        pack_kernel,
        out_shape=jax.ShapeDtypeStruct((n, tok_rows, 2 * gate_rows + LANES), jnp.bfloat16),
        in_specs=[vmem()] * 3,
        out_specs=vmem(),
        compiler_params=params(62),
    )(tokens, expert_ids.T, gate_weights.T)
    got = lax.all_to_all(packed, "ep", split_axis=0, concat_axis=0, tiled=True)
    got = got.reshape(all_tokens, 2 * gate_rows + LANES)

    group = 8 if n % 8 == 0 else 4
    per_half = n // group
    block = pl.BlockSpec((group // 2, down_rows, depth), lambda i: (i, 0, 0))
    half_shape = jax.ShapeDtypeStruct((n // 2, down_rows, depth), jnp.bfloat16)
    own, pair = [], []
    for half in range(2):
        send, keep = pl.pallas_call(
            prep_kernel,
            grid=(per_half,),
            out_shape=(half_shape,) * 2,
            in_specs=[
                smem(),
                pl.BlockSpec(
                    (gate_rows, experts, group * down_rows),
                    lambda i, half=half: (0, 0, half * per_half + i),
                ),
            ],
            out_specs=(block,) * 2,
            compiler_params=params(PREP_MIB),
            cost_estimate=pl.CostEstimate(
                flops=gate_up.size, bytes_accessed=2 * gate_up.size, transcendentals=0
            ),
        )(me, gate_up)
        pair.append(lax.ppermute(send, "ep", [(i, i ^ 1) for i in range(n)]))
        own.append(keep)

    blocks = BLOCKS if (n // 2) % BLOCKS == 0 else 2
    steps = n // 2 // blocks
    groups = GROUPS if len(plan) == sum(GROUPS) else (1,) * len(plan)
    all_pieces, c = [], 0
    for group in groups:
        first_k = sum(chunks[:c])
        parts = [(size, bit_order(bits - 1, turn)) for size, turn in plan[c : c + group]]
        lanes = sum(size for size, _ in parts) * all_tokens
        out_shape = []
        for size, _ in parts:
            shape = (n // 4, 2 * down_rows, size * all_tokens)
            out_shape.append(jax.ShapeDtypeStruct(shape, jnp.bfloat16))
            out_shape.append(jax.ShapeDtypeStruct(shape, jnp.float32))
        out_specs = [pl.BlockSpec(o.shape, lambda i: (0, 0, 0)) for o in out_shape]
        part = (steps, 2 * blocks * down_rows, lanes)
        part_spec = pl.BlockSpec((1,) + part[1:], lambda i: (i, 0, 0))

        def hidden(sides, weights, base, out_shape, out_specs):
            return pl.pallas_call(
                functools.partial(
                    hidden_kernel, first_k, parts, top, experts, sides, len(base) == 1
                ),
                grid=(steps,),
                out_shape=out_shape,
                in_specs=[smem(), vmem()]
                + [pl.BlockSpec((blocks, down_rows, depth), lambda i: (i, 0, 0))]
                * len(weights)
                + [part_spec] * len(base),
                out_specs=out_specs,
                scratch_shapes=[pltpu.VMEM((gate_rows, experts, lanes), jnp.bfloat16)]
                * len(sides),
                compiler_params=params(HID_MIB),
                cost_estimate=pl.CostEstimate(
                    flops=depth * gate_cols * lanes * len(sides),
                    bytes_accessed=depth * gate_cols * len(sides)
                    + 3 * gate_cols * lanes // 2,
                    transcendentals=0,
                ),
            )(me, got, *weights, *base)

        if c:
            made = hidden((0, 1), own + pair, [], out_shape, out_specs)
        else:
            base = hidden((0,), own, [], jax.ShapeDtypeStruct(part, jnp.float32), part_spec)
            made = hidden((1,), pair, [base], out_shape, out_specs)
        for at, (_, order) in enumerate(parts):
            send, keep = made[2 * at : 2 * at + 2]
            all_pieces += [keep] + scatter(send, [keep], n, 1, order, add_up)
            c += 1

    parts = len(all_pieces) // len(chunks)
    scale_cols = gate_cols + model_width
    steps = OUT_STEPS if model_width % (OUT_STEPS * LANES) == 0 else 2
    base = tok_rows * model_width // LANES // steps
    extra = -(-scale_cols // (8 * steps * LANES)) * 8
    gate_max = column_max(gate_up, 2)
    down_max = column_max(down_proj, 2)
    local_max = jnp.concatenate(
        [
            gate_max,
            down_max,
            jnp.zeros((experts, steps * extra * LANES - scale_cols), jnp.bfloat16),
        ],
        axis=1,
    ).reshape(experts, steps, extra, LANES)

    early, late = all_pieces[:-parts], all_pieces[-parts:]
    before = pl.pallas_call(
        functools.partial(left_kernel, chunks[:-1], parts, top, experts),
        grid=(1,),
        out_shape=jax.ShapeDtypeStruct((down_rows, experts, all_tokens), jnp.bfloat16),
        in_specs=[vmem()] + [first_slot(p) for p in early],
        out_specs=vmem(),
        compiler_params=params(16),
    )(got, *early)
    orders = [(0,) + tuple(b + 1 for b in bit_order(bits - 1, turn)) for turn in range(2)]
    shape = (n // 2, steps * (base + extra), LANES)
    out_block = pl.BlockSpec((n // 2, base + extra, LANES), lambda i: (0, i, 0))
    send, keep = pl.pallas_call(
        functools.partial(
            down_kernel, chunks[-1], top - chunks[-1], parts, top, experts, base, orders
        ),
        grid=(steps,),
        out_shape=(jax.ShapeDtypeStruct(shape, jnp.float32),) * 2,
        in_specs=[
            smem(),
            smem(),
            vmem(),
            vmem(),
            pl.BlockSpec((down_rows * experts, model_width // steps), lambda i: (0, i)),
            pl.BlockSpec((experts, 1, extra, LANES), lambda i: (0, i, 0, 0)),
        ]
        + [first_slot(p) for p in late],
        out_specs=(out_block,) * 2,
        scratch_shapes=[
            pltpu.VMEM((all_tokens, down_rows * experts), jnp.bfloat16),
            pltpu.VMEM((all_tokens, model_width // steps), jnp.float32),
            pltpu.SMEM((n,), jnp.int32),
        ],
        compiler_params=params(20),
    )(
        me,
        owner_slot,
        got,
        before,
        down_proj.reshape(down_rows * experts, model_width),
        local_max,
        *late,
    )

    def merge(terms):
        row = lax.broadcasted_iota(jnp.int32, terms[0].shape, 1) % (base + extra)
        terms = [t.astype(jnp.float32) for t in terms]
        return jnp.where(row < base, sum(terms), functools.reduce(jnp.maximum, terms)).astype(
            jnp.bfloat16
        )

    pieces = [keep] + scatter(send, [keep], n, 0, (0,), merge)
    middle = steps // 2 * (base + extra)
    for half, order in enumerate(orders):
        own = [p[:, half * middle : (half + 1) * middle] for p in pieces[:2]]
        pieces = pieces + scatter(None, own, n, 0, order[1:], merge)
    return pl.pallas_call(
        functools.partial(
            finish_kernel,
            gate_cols,
            math.sqrt(gate_rows * n),
            math.sqrt(down_rows * n),
            base,
            extra,
            bits - 1,
        ),
        grid=(1,),
        out_shape=(
            jax.ShapeDtypeStruct((tok_rows, model_width), jnp.bfloat16),
            jax.ShapeDtypeStruct((1, scale_cols), jnp.float32),
        ),
        in_specs=[first_slot(p) for p in pieces],
        out_specs=(vmem(),) * 2,
        compiler_params=params(10),
    )(*pieces)


def shards(tokens, gate_up, down_proj, expert_ids, gate_weights, owner_slot):
    n = lax.axis_size("ep")
    tok_rows, model_width = tokens.shape
    top = expert_ids.shape[1]
    gate_rows, experts, gate_cols = gate_up.shape
    down_rows = down_proj.shape[0]
    fits = (
        n >= 2
        and n & (n - 1) == 0
        and experts == n
        and experts % 16 == 0
        and tok_rows % 16 == 0
        and gate_rows % LANES == 0
        and down_rows % 16 == 0
        and n % 4 == 0
        and model_width % LANES == 0
        and gate_cols % LANES == 0
        and 3 * top <= LANES
        and experts <= 256
    )
    path = row_shards if fits else owner_shards
    return path(tokens, gate_up, down_proj, expert_ids, gate_weights, owner_slot)


def solution(mesh):
    in_specs = (
        P(("parts", "ep"), None),
        P(("parts", "ep"), None, None),
        P(("parts", "ep"), None, None),
        P(("parts", "ep"), None),
        P(("parts", "ep"), None),
        P("parts"),
    )
    out_specs = (P(("parts", "ep"), None), P(("parts", "ep"), None))
    return jax.shard_map(
        shards, mesh=mesh, in_specs=in_specs, out_specs=out_specs, check_vma=False
    )
```
